32 devices in a mesh: group: 4 (over z), dev: 8 (over y, x, core).
Axes of the slice: x: 2, y: 2, z: 4, core: 2. Of those that a mesh axis runs over, the one named last changes fastest.
Arguments:
- tile_values: bfloat16 [512, 128, 128], P(('group', 'dev')), may hold values from -0.25 to 0.25
- tile_rows: int32 [512], P(('group', 'dev')), may hold values from 0 to 1
- tile_columns: int32 [512], P(('group', 'dev')), may hold values from 0 to 15
- tile_count: int32 [32], P(('group', 'dev')), may hold values from 4 to 16, as said below
- start_basis: bfloat16 [8192, 64], P(('group', 'dev')), may hold values from -6 to 6
- seed_rows: int32 [1024], replicated, may hold values from 0 to 8191
Outputs:
- unit_embedding: float32 [8192, 64], P(('group', 'dev'))
- centroids: float32 [1024, 64], replicated
The draws below stay inside these ranges and needn't reach their ends.
Inputs may be any that keep to these rules, and one draw needn't show every extreme that they name: `tile_count`: the most, 16, is reached by some device in every draw.
All inputs are finite; a program needn't handle non-finite values.
Results may differ from the reference program's by a relative error of at most 0.0029.
Values may be sent and summed in bfloat16 or wider, within the bound.
A program may use at most 64 MiB of HBM per device.

```python
import jax
import jax.numpy as jnp
from jax import lax

BLOCK = 128
BASIS = 64
CLUSTERS = 1024
ROWS_DEV = 256
TILES_MAX = 16
ITERS = 2
KSTEPS = 2
ROW_BLOCKS = 2
GROUP_BLOCKS = 16
NROWS = 8192
N_GROUP = 4
N_DEV = 8
DEVICES = 32


def draw_tile_count(key, part):
    first_key, second_key, third_key = jax.random.split(jax.random.fold_in(key, 17), 3)
    device_total = N_GROUP * N_DEV
    base = jax.random.randint(first_key, (device_total,), TILES_MAX // 4, TILES_MAX // 2 + 1)
    full = jax.random.randint(second_key, (device_total,), 0, 8) == 0
    counts = jnp.where(full, TILES_MAX, base)
    chosen = jax.random.randint(third_key, (), 0, device_total)
    return counts.at[chosen].set(TILES_MAX).astype(jnp.int32)


def touch_ends(array, key, smallest, top_value):
    place = [jax.random.randint(jax.random.fold_in(key, axis), (), 0, length) for axis, length in enumerate(array.shape)]
    main_axis = array.shape.index(max(array.shape))
    beside = place[:main_axis] + [(place[main_axis] + 1) % array.shape[main_axis]] + place[main_axis + 1:]
    return array.at[tuple(place)].set(smallest).at[tuple(beside)].set(top_value)


def block_scale(stream_key, shape, cuts, least, top_value):
    factor_of = 1.0
    for dim, blocks in cuts:
        draws = jax.random.uniform(jax.random.fold_in(jax.random.fold_in(stream_key, 6), dim), (blocks,), jnp.float32, least / len(cuts), top_value / len(cuts))
        factor_of = factor_of * jnp.repeat(jnp.exp(draws), shape[dim] // blocks).reshape((-1,) + (1,) * (len(shape) - 1 - dim))
    return factor_of


def gaussian(rng, shape, width, most, pieces=(), kind=jnp.bfloat16):
    array = jax.random.normal(rng, shape, jnp.float32) * width
    if len(pieces) > 0:
        array = block_scale(rng, shape, pieces, -0.22, 0.18) * array
    return jnp.clip(array, min=-most, max=most).astype(kind)


def setup_inputs(seed: int = 0) -> dict:
    arg_keys = jax.random.split(jax.random.key(seed), 7)
    tile_values = gaussian(arg_keys[0], (DEVICES * TILES_MAX, BLOCK, BLOCK), (4 * BLOCK) ** -0.5, 0.25, ((0, 32),))
    tile_rows = touch_ends(jax.random.randint(arg_keys[1], (DEVICES * TILES_MAX,), 0, ROW_BLOCKS), jax.random.fold_in(arg_keys[1], 1), 0, ROW_BLOCKS - 1).astype(jnp.int32)
    tile_columns = touch_ends(jax.random.randint(arg_keys[2], (DEVICES * TILES_MAX,), 0, GROUP_BLOCKS), jax.random.fold_in(arg_keys[2], 1), 0, GROUP_BLOCKS - 1).astype(jnp.int32)
    tile_count = draw_tile_count(jax.random.fold_in(arg_keys[6], 71), 0)
    start_basis = gaussian(arg_keys[4], (NROWS, BASIS), 1.0, 6.0, ((0, 32),))
    seed_rows = touch_ends(jax.random.randint(arg_keys[5], (CLUSTERS,), 0, NROWS), jax.random.fold_in(arg_keys[5], 1), 0, NROWS - 1).astype(jnp.int32)
    return {"tile_values": tile_values, "tile_rows": tile_rows, "tile_columns": tile_columns, "tile_count": tile_count, "start_basis": start_basis, "seed_rows": seed_rows}


def apply_tiles(tile_block, row_index, column_index, live_count, group_basis):
    basis_blocks = group_basis.reshape(-1, BLOCK, BASIS)
    picked = jnp.take(basis_blocks, column_index, axis=0)
    products = jnp.einsum('tij,tjk->tik', tile_block.astype(jnp.float32), picked.astype(jnp.float32))
    live = jnp.arange(TILES_MAX, dtype=jnp.int32) < live_count
    block_index = jnp.arange(ROWS_DEV // BLOCK, dtype=jnp.int32)
    select = ((row_index[None, :] == block_index[:, None]) & live[None, :]).astype(jnp.float32)
    total = jnp.einsum('rt,tik->rik', select, products)
    return total.reshape(ROWS_DEV, BASIS)

def reference(tile_values, tile_rows, tile_columns, tile_count, start_basis, seed_rows):
    device_total = N_GROUP * N_DEV
    tiles_each = tile_values.reshape(device_total, TILES_MAX, BLOCK, BLOCK)
    rows_each = tile_rows.reshape(device_total, TILES_MAX)
    columns_each = tile_columns.reshape(device_total, TILES_MAX)
    basis = start_basis
    embedding = None
    for step_index in range(ITERS):
        group_basis = basis.reshape(N_GROUP, N_DEV * ROWS_DEV, BASIS)

        def one_device(device):
            return apply_tiles(tiles_each[device], rows_each[device], columns_each[device], tile_count[device], group_basis[device // N_DEV])
        image = lax.map(one_device, jnp.arange(device_total, dtype=jnp.int32)).reshape(NROWS, BASIS)
        gram = jnp.dot(image.T, image, precision=lax.Precision.HIGHEST)
        lower = jnp.linalg.cholesky(gram)
        solved = lax.linalg.triangular_solve(lower, image, left_side=False, lower=True, transpose_a=True)
        if step_index + 1 < ITERS:
            basis = solved.astype(jnp.bfloat16)
        else:
            embedding = solved * jnp.sqrt(jnp.float32(NROWS))
    unit = embedding / jnp.sqrt(lax.optimization_barrier(jnp.sum(embedding * embedding, axis=1, keepdims=True)) + 1e-06)
    centres = unit[seed_rows]
    unit_blocks = unit.reshape(-1, ROWS_DEV, BASIS)
    for kstep in range(KSTEPS):
        centre_square = lax.optimization_barrier(jnp.sum(centres * centres, axis=1))

        def accumulate(carry, rows_block):
            weighted, mass = carry
            dist = lax.optimization_barrier(jnp.sum(rows_block * rows_block, axis=1))[:, None] - 2.0 * jnp.dot(rows_block, centres.T, precision=lax.Precision.HIGHEST) + centre_square[None, :]
            weights = jnp.exp(-4.0 * dist)
            member = weights / lax.optimization_barrier(jnp.sum(weights, axis=1, keepdims=True))
            weighted = weighted + jnp.dot(member.T, rows_block, precision=lax.Precision.HIGHEST)
            mass = mass + lax.optimization_barrier(jnp.sum(member, axis=0))
            return ((weighted, mass), None)
        start = (jnp.zeros((CLUSTERS, BASIS), jnp.float32), jnp.zeros((CLUSTERS,), jnp.float32))
        (weighted, mass), unused = lax.scan(accumulate, start, unit_blocks)
        centres = weighted / mass[:, None]
    return (unit, centres)
```

```python
import functools

import jax
import jax.numpy as jnp
from jax import lax
from jax.experimental import pallas as pl
from jax.experimental.pallas import tpu as pltpu
from jax.sharding import PartitionSpec as P

KSTEPS = 2
SHARPNESS = 4.0
MASS_ROWS = 16
LANES = 128
MESH = pl.DeviceIdType.MESH
F32 = jnp.float32
HIGHEST = lax.Precision.HIGHEST
NN = (((1,), (0,)), ((), ()))
NT = (((1,), (1,)), ((), ()))
TN = (((0,), (0,)), ((), ()))


def mm(a, b, dims=NN):
    return lax.dot_general(a, b, dims, precision=HIGHEST, preferred_element_type=F32)


def high_low(x):
    high = x.astype(jnp.bfloat16)
    return high, (x - high.astype(F32)).astype(jnp.bfloat16)


def dot16(a, b, dims=NN):
    return lax.dot_general(a, b, dims, preferred_element_type=F32)


def three(x):
    high = x.astype(jnp.bfloat16)
    return (high, *high_low(x - high.astype(F32)))


def loop(n, body):
    if n <= 8:
        for i in range(n):
            body(i)
    else:

        def step(i, carry):
            body(i)
            return carry

        lax.fori_loop(0, n, step, 0)


def fold(n, ref):
    total = ref[0].astype(F32)
    if n <= 8:
        for i in range(1, n):
            total = total + ref[i].astype(F32)
        return total
    return lax.fori_loop(1, n, lambda i, total: total + ref[i].astype(F32), total)


class Exchange:
    def __init__(self, axis, n, me, land, sems, source=None):
        self.axis, self.n, self.me = axis, n, me
        self.land, self.source = land, source
        self.send, self.recv = sems

    def copy(self, peer, slot):
        source = self.land(self.me) if self.source is None else self.source(peer)
        return pltpu.make_async_remote_copy(
            src_ref=source,
            dst_ref=self.land(slot),
            send_sem=self.send.at[peer],
            recv_sem=self.recv.at[slot],
            device_id={self.axis: peer},
            device_id_type=MESH,
        )

    def peer(self, i):
        return lax.rem(self.me + 1 + i, self.n)

    def start(self):
        loop(self.n - 1, lambda i: self.copy(self.peer(i), self.me).start())

    def wait_recv(self):
        loop(self.n - 1, lambda i: self.copy(self.peer(i), self.peer(i)).wait_recv())

    def wait_send(self):
        loop(self.n - 1, lambda i: self.copy(self.peer(i), self.me).wait_send())


def total_of(n, value):
    total = value(0)
    if n <= 8:
        for d in range(1, n):
            total = total + value(d)
        return total
    return lax.fori_loop(1, n, lambda d, total: total + value(d), total)


class Gather:
    def __init__(self, n, me, land, pairs):
        self.n, self.me, self.land = n, me, land
        self.pairs = pairs
        self.twin = self.me + 1 - 2 * lax.rem(self.me, 2)

    def copy(self, owner, slot, to, stage):
        send, recv = self.pairs[stage]
        return pltpu.make_async_remote_copy(
            src_ref=self.land(owner),
            dst_ref=self.land(owner),
            send_sem=send.at[slot],
            recv_sem=recv.at[owner],
            device_id={"dev": to},
            device_id_type=MESH,
        )

    def far(self, i):
        return lax.rem(self.me + 2 + 2 * i, self.n)

    def start(self):
        self.copy(self.me, self.me, self.twin, 1).start()
        loop(self.n // 2 - 1, lambda i: self.copy(self.me, self.far(i), self.far(i), 0).start())

    def relay(self):
        def one(i):
            owner = self.far(i)
            self.copy(owner, owner, owner, 0).wait_recv()
            self.copy(owner, owner, self.twin, 1).start()

        loop(self.n // 2 - 1, one)

    def other(self, i):
        return lax.rem(self.twin + 2 * i, self.n)

    def wait_recv(self):
        loop(self.n // 2, lambda i: self.copy(self.other(i), self.other(i), self.twin, 1).wait_recv())

    def wait_send(self):
        self.copy(self.me, self.me, self.twin, 1).wait_send()

        def one(i):
            owner = self.far(i)
            self.copy(self.me, owner, owner, 0).wait_send()
            self.copy(owner, owner, self.twin, 1).wait_send()

        loop(self.n // 2 - 1, one)


def factor_inverse(gram):
    k = gram.shape[0]
    wide = 2 * k
    rows = lax.broadcasted_iota(jnp.int32, (k, k), 0)
    lanes = lax.broadcasted_iota(jnp.int32, (k, k), 1)
    table = jnp.concatenate([gram, jnp.where(rows == lanes, 1.0, 0.0).astype(F32)], axis=1)
    count = k // 8
    parts = [table[8 * b : 8 * b + 8] for b in range(count)]
    sub = lax.broadcasted_iota(jnp.int32, (8, wide), 0)

    def full(v):
        return jnp.broadcast_to(v, (8, wide))

    done = []
    for b in range(count):
        own, at = parts[b], 8 * b
        row = [full(own[s : s + 1]) for s in range(8)]
        cell = [[full(own[s : s + 1, at + r : at + r + 1]) for r in range(s + 1)] for s in range(8)]
        column = {c: [full(parts[c][:, at + r : at + r + 1]) for r in range(8)] for c in range(b + 1, count)}
        over = []
        for r in range(8):
            over.append(1.0 / cell[r][r])
            for s in range(r + 1, 8):
                ratio = cell[s][r] * over[r]
                for t in range(r + 1, s + 1):
                    cell[s][t] = cell[s][t] - ratio * cell[t][r]
                row[s] = row[s] - ratio * row[r]
                for values in column.values():
                    values[s] = values[s] - ratio * values[r]
        for c, values in column.items():
            for r in range(8):
                parts[c] = parts[c] - values[r] * (row[r] * over[r])
        own = row[0] / jnp.sqrt(cell[0][0])
        for s in range(1, 8):
            own = jnp.where(sub == s, row[s] / jnp.sqrt(cell[s][s]), own)
        done.append(own)
    return jnp.concatenate(done, axis=0)[:, k:]


def pack(gram):
    half = gram.shape[0] // 2
    return jnp.concatenate([gram[:half], gram[half:]], axis=1)


def unpack(packed):
    k = packed.shape[1] // 2
    return jnp.concatenate([packed[:, :k], packed[:, k:]], axis=0)


def kernel(
    n, m, total_rows,
    tiles_in, rows_in, columns_in, count_in, start_in, seeds_in,
    unit_out, centres_out,
    tiles, rows_ref, columns_ref, count_ref, seeds,
    matrix, basis0, basis1, images0, images1, gram_dev, gram_group,
    chooser, seed_group, right, left, square, units, weights, den, weights_scale, sums, final,
    in_sems, out_sems, *sems,
):
    me, g = lax.axis_index("dev"), lax.axis_index("group")
    pairs = [(sems[2 * i], sems[2 * i + 1]) for i in range(len(sems) // 2)]
    slots, block = tiles.shape[0], tiles.shape[1]
    width, local_rows = start_in.shape
    row_blocks = local_rows // block
    part = seeds.shape[1]

    barrier = pltpu.get_barrier_semaphore()
    for axis, size, index in (("dev", n, me), ("group", m, g)):
        loop(
            size - 1,
            lambda i: pl.semaphore_signal(
                barrier, inc=1, device_id={axis: lax.rem(index + 1 + i, size)}, device_id_type=MESH
            ),
        )
    loads = [(start_in.at[:, r * block : (r + 1) * block], basis0.at[me * row_blocks + r]) for r in range(row_blocks)]
    loads += [(rows_in, rows_ref), (columns_in, columns_ref), (count_in, count_ref), (seeds_in.at[me], seeds)]
    loads += [(tiles_in, tiles)]
    loads = [pltpu.make_async_copy(a, b, in_sems.at[i]) for i, (a, b) in enumerate(loads)]
    for load in loads:
        load.start()
    for load in loads:
        load.wait()
    pl.semaphore_wait(barrier, n - 1 + m - 1)

    used = iter(pairs)
    pending = []

    def exchange(axis, land, source=None):
        size, index = (n, me) if axis == "dev" else (m, g)
        made = Exchange(axis, size, index, land, next(used), source)
        made.start()
        pending.append(made)
        return made

    gather = exchange("dev", lambda d: basis0.at[pl.ds(d * row_blocks, row_blocks)])
    count = count_ref[0, 0]
    for s in range(slots):
        for r in range(row_blocks):
            keep = jnp.logical_and(rows_ref[s] == r, s < count)
            matrix[r * block : (r + 1) * block, s * block : (s + 1) * block] = tiles[s] * jnp.where(
                keep, 1.0, 0.0
            ).astype(jnp.bfloat16)

    def choose(d):
        first_row = (g * n + d) * local_rows
        chooser[d] = jnp.where(
            lax.broadcasted_iota(jnp.int32, (local_rows, part), 0) == seeds[...] - first_row, 1.0, 0.0
        ).astype(jnp.bfloat16)
        right[d, 3 * width :] = jnp.ones((MASS_ROWS, local_rows), jnp.bfloat16)
        left[d, 2 * width :] = jnp.ones((MASS_ROWS, local_rows), jnp.bfloat16)

    loop(n, choose)

    def apply(basis):
        picked = jnp.concatenate([basis[columns_ref[s]] for s in range(slots)], axis=1)
        return lax.dot_general(picked, matrix[...], NT, preferred_element_type=F32)

    def start_gram(image, turn):
        gram_dev[turn, me] = pack(mm(image, image, NT))
        return exchange("dev", lambda d: gram_dev.at[turn, d])

    def end_gram(first, turn):
        first.wait_recv()
        gram_group[turn, g] = fold(n, gram_dev.at[turn])
        return exchange("group", lambda d: gram_group.at[turn, d])

    gather.wait_recv()
    image = apply(basis0)
    first = start_gram(image, 0)
    images0[me] = image
    gather = exchange("dev", lambda d: images0.at[d])
    second = end_gram(first, 0)
    second.wait_recv()
    inverse = factor_inverse(unpack(fold(m, gram_group.at[0])))
    gather.wait_recv()

    def solve(d):
        solved = mm(inverse, images0[d])
        for r in range(row_blocks):
            basis1[d * row_blocks + r] = solved[:, r * block : (r + 1) * block].astype(jnp.bfloat16)

    loop(n, solve)
    image = apply(basis1)
    first = start_gram(image, 1)
    images1[me] = image
    gather = Gather(n, me, lambda d: images1.at[d], [next(used) for _ in range(2)])
    gather.start()
    second = end_gram(first, 1)
    gather.relay()
    gather.wait_recv()

    def chosen(d):
        pieces = dot16(jnp.concatenate(three(images1[d]), axis=0), chooser[d])
        return pieces[:width] + pieces[width : 2 * width] + pieces[2 * width :]

    seed_group[g] = total_of(n, chosen)
    seeding = exchange("group", lambda d: seed_group.at[d])
    second.wait_recv()
    inverse = factor_inverse(unpack(fold(m, gram_group.at[1])))

    def normalise(image_t):
        embedding = mm(inverse, image_t) * jnp.sqrt(F32(total_rows))
        return embedding / jnp.sqrt(jnp.sum(embedding * embedding, axis=0, keepdims=True) + 1e-06)

    def embed(d):
        unit = normalise(images1[d])
        units[d] = unit
        square[d] = -SHARPNESS * jnp.sum(unit * unit, axis=0, keepdims=True)
        high, low = high_low(unit)
        for at, piece in enumerate((high, low, high)):
            right[d, at * width : (at + 1) * width] = piece
        left[d, :width] = high
        left[d, width : 2 * width] = low

    loop(n, embed)
    unit_copy = pltpu.make_async_copy(units.at[me], unit_out, out_sems.at[0])
    unit_copy.start()
    seeding.wait_recv()
    centres = normalise(fold(m, seed_group))
    for turn in range(KSTEPS):
        high, low = high_low(2.0 * SHARPNESS * centres)
        bias = [v.astype(F32) for v in three(-SHARPNESS * jnp.sum(centres * centres, axis=0, keepdims=True))]
        bias = jnp.concatenate([*bias, jnp.zeros((MASS_ROWS - len(bias), part), F32)], axis=0).astype(jnp.bfloat16)
        table = jnp.concatenate([high, high, low, bias], axis=0)

        def weigh(d):
            values = jnp.exp(dot16(table, right[d], TN) + square[d])
            weights[d] = values
            den[turn, me, pl.ds(d, 1)] = jnp.sum(values, axis=0, keepdims=True)

        loop(n, weigh)
        exchange("dev", lambda d: den.at[turn, d]).wait_recv()
        units_of = 1.0 / fold(n, den.at[turn])
        weights_scale[...] = units_of

        def gathered(d):
            member = weights[d] * weights_scale[pl.ds(d, 1)]
            return dot16(left[d], member.astype(jnp.bfloat16), NT)

        pair = total_of(n, gathered)
        mass = pair[2 * width : 2 * width + 1]
        sums[turn, g, :width] = pair[:width] + pair[width : 2 * width]
        sums[turn, g, width:] = jnp.broadcast_to(mass, (8, part))
        exchange("group", lambda d: sums.at[turn, d]).wait_recv()
        total = fold(m, sums.at[turn])
        centres = total[:width] / total[width : width + 1]
    final[...] = centres.astype(jnp.bfloat16)
    own_copy = pltpu.make_async_copy(final, centres_out.at[me], out_sems.at[1])
    own_copy.start()
    exchange("dev", lambda d: centres_out.at[d], lambda p: final).wait_recv()
    own_copy.wait()
    unit_copy.wait()
    for made in pending:
        made.wait_send()
    gather.wait_send()


def local(tile_values, tile_rows, tile_columns, tile_count, start_basis, seed_rows):
    n, m = lax.axis_size("dev"), lax.axis_size("group")
    slots, block = tile_values.shape[0], tile_values.shape[1]
    local_rows, width = start_basis.shape
    row_blocks = local_rows // block
    clusters = seed_rows.shape[0]
    part = clusters // n
    anywhere = pl.BlockSpec(memory_space=pl.ANY)
    half = (width // 2, 2 * width)
    B16 = jnp.bfloat16
    axes = ["dev", "dev", "dev", "group", "dev", "dev", "dev", "group", "group"]
    axes += ["dev", "group"] * KSTEPS + ["dev"]
    sems = []
    for axis in axes:
        sems += [pltpu.SemaphoreType.DMA((n if axis == "dev" else m,))] * 2
    unit, centres = pl.pallas_call(
        functools.partial(kernel, n, m, local_rows * n * m),
        out_shape=(
            jax.ShapeDtypeStruct((width, local_rows), F32),
            jax.ShapeDtypeStruct((n, width, part), B16),
        ),
        in_specs=[anywhere] * 6,
        out_specs=(anywhere, anywhere),
        scratch_shapes=[
            pltpu.VMEM(tile_values.shape, B16),
            pltpu.SMEM(tile_rows.shape, jnp.int32),
            pltpu.SMEM(tile_columns.shape, jnp.int32),
            pltpu.SMEM((1, 1), jnp.int32),
            pltpu.VMEM((1, part), jnp.int32),
            pltpu.VMEM((local_rows, slots * block), B16),
            pltpu.VMEM((n * row_blocks, width, block), B16),
            pltpu.VMEM((n * row_blocks, width, block), B16),
            pltpu.VMEM((n, width, local_rows), F32),
            pltpu.VMEM((n, width, local_rows), F32),
            pltpu.VMEM((2, n, *half), F32),
            pltpu.VMEM((2, m, *half), F32),
            pltpu.VMEM((n, local_rows, part), B16),
            pltpu.VMEM((m, width, part), F32),
            pltpu.VMEM((n, 3 * width + MASS_ROWS, local_rows), B16),
            pltpu.VMEM((n, 2 * width + MASS_ROWS, local_rows), B16),
            pltpu.VMEM((n, 1, local_rows), F32),
            pltpu.VMEM((n, width, local_rows), F32),
            pltpu.VMEM((n, part, local_rows), F32),
            pltpu.VMEM((KSTEPS, n, n, local_rows), F32),
            pltpu.VMEM((n, local_rows), F32),
            pltpu.VMEM((KSTEPS, m, width + 8, part), F32),
            pltpu.VMEM((width, part), B16),
            pltpu.SemaphoreType.DMA((row_blocks + 5,)),
            pltpu.SemaphoreType.DMA((2,)),
            *sems,
        ],
        compiler_params=pltpu.CompilerParams(
            collective_id=0, has_side_effects=True, vmem_limit_bytes=58 * 1024 * 1024
        ),
        name="spectral",
    )(tile_values, tile_rows, tile_columns, tile_count.reshape(1, 1), start_basis.T, seed_rows.reshape(n, 1, part))
    return unit.T, centres.transpose(0, 2, 1).reshape(clusters, width).astype(F32)


def solution(mesh):
    return jax.shard_map(
        local,
        mesh=mesh,
        in_specs=(
            P(("group", "dev"), None, None),
            P(("group", "dev")),
            P(("group", "dev")),
            P(("group", "dev")),
            P(("group", "dev"), None),
            P(),
        ),
        out_specs=(P(("group", "dev"), None), P()),
        check_vma=False,
    )
```

```python
import functools

import jax
import jax.numpy as jnp
from jax import lax
from jax.experimental import pallas as pl
from jax.experimental.pallas import tpu as pltpu
from jax.sharding import PartitionSpec as P

KSTEPS = 2
SHARPNESS = 4.0
MASS_ROWS = 16
LANES = 128
MESH = pl.DeviceIdType.MESH
F32 = jnp.float32
HIGHEST = lax.Precision.HIGHEST
NN = (((1,), (0,)), ((), ()))
NT = (((1,), (1,)), ((), ()))
TN = (((0,), (0,)), ((), ()))


def mm(a, b, dims=NN):
    return lax.dot_general(a, b, dims, precision=HIGHEST, preferred_element_type=F32)


def high_low(x):
    high = x.astype(jnp.bfloat16)
    return high, (x - high.astype(F32)).astype(jnp.bfloat16)


def dot16(a, b, dims=NN):
    return lax.dot_general(a, b, dims, preferred_element_type=F32)


def three(x):
    high = x.astype(jnp.bfloat16)
    return (high, *high_low(x - high.astype(F32)))


def loop(n, body):
    if n <= 8:
        for i in range(n):
            body(i)
    else:

        def step(i, carry):
            body(i)
            return carry

        lax.fori_loop(0, n, step, 0)


def fold(n, ref):
    total = ref[0].astype(F32)
    if n <= 8:
        for i in range(1, n):
            total = total + ref[i].astype(F32)
        return total
    return lax.fori_loop(1, n, lambda i, total: total + ref[i].astype(F32), total)


def flip(me, mask):
    out, bit = me, 1
    while bit <= mask:
        if mask & bit:
            out = out + bit - 2 * bit * lax.rem(out // bit, 2)
        bit *= 2
    return out


class Exchange:
    def __init__(self, axis, n, me, land, sems, source=None):
        self.axis, self.n, self.me = axis, n, me
        self.land, self.source = land, source
        self.send, self.recv = sems

    def copy(self, peer, slot):
        source = self.land(self.me) if self.source is None else self.source(peer)
        return pltpu.make_async_remote_copy(
            src_ref=source,
            dst_ref=self.land(slot),
            send_sem=self.send.at[peer],
            recv_sem=self.recv.at[slot],
            device_id={self.axis: peer},
            device_id_type=MESH,
        )

    def peer(self, i):
        if self.n <= 8 and self.n & (self.n - 1) == 0:
            return flip(self.me, self.n - 1 - i)
        return lax.rem(self.me + 1 + i, self.n)

    def start(self):
        loop(self.n - 1, lambda i: self.copy(self.peer(i), self.me).start())

    def wait_recv(self):
        loop(self.n - 1, lambda i: self.copy(self.peer(i), self.peer(i)).wait_recv())

    def wait_send(self):
        loop(self.n - 1, lambda i: self.copy(self.peer(i), self.me).wait_send())


def total_of(n, value):
    total = value(0)
    if n <= 8:
        for d in range(1, n):
            total = total + value(d)
        return total
    return lax.fori_loop(1, n, lambda d, total: total + value(d), total)


class Gather:
    def __init__(self, n, me, land, pairs):
        self.n, self.me, self.land = n, me, land
        self.pairs = pairs
        self.twin = self.me + 1 - 2 * lax.rem(self.me, 2)

    def copy(self, owner, slot, to, stage):
        send, recv = self.pairs[stage]
        return pltpu.make_async_remote_copy(
            src_ref=self.land(owner),
            dst_ref=self.land(owner),
            send_sem=send.at[slot],
            recv_sem=recv.at[owner],
            device_id={"dev": to},
            device_id_type=MESH,
        )

    def far(self, i):
        return lax.rem(self.me + 2 + 2 * i, self.n)

    def start(self):
        self.copy(self.me, self.me, self.twin, 1).start()
        loop(self.n // 2 - 1, lambda i: self.copy(self.me, self.far(i), self.far(i), 0).start())

    def relay(self):
        def one(i):
            owner = self.far(i)
            self.copy(owner, owner, owner, 0).wait_recv()
            self.copy(owner, owner, self.twin, 1).start()

        loop(self.n // 2 - 1, one)

    def other(self, i):
        return lax.rem(self.twin + 2 * i, self.n)

    def wait_recv(self):
        loop(self.n // 2, lambda i: self.copy(self.other(i), self.other(i), self.twin, 1).wait_recv())

    def wait_send(self):
        self.copy(self.me, self.me, self.twin, 1).wait_send()

        def one(i):
            owner = self.far(i)
            self.copy(self.me, owner, owner, 0).wait_send()
            self.copy(owner, owner, self.twin, 1).wait_send()

        loop(self.n // 2 - 1, one)


def factor_inverse(gram):
    k = gram.shape[0]
    wide = 2 * k
    rows = lax.broadcasted_iota(jnp.int32, (k, k), 0)
    lanes = lax.broadcasted_iota(jnp.int32, (k, k), 1)
    table = jnp.concatenate([gram, jnp.where(rows == lanes, 1.0, 0.0).astype(F32)], axis=1)
    count = k // 8
    parts = [table[8 * b : 8 * b + 8] for b in range(count)]
    sub = lax.broadcasted_iota(jnp.int32, (8, wide), 0)

    def full(v):
        return jnp.broadcast_to(v, (8, wide))

    done = []
    for b in range(count):
        own, at = parts[b], 8 * b
        row = [full(own[s : s + 1]) for s in range(8)]
        cell = [[full(own[s : s + 1, at + r : at + r + 1]) for r in range(s + 1)] for s in range(8)]
        column = {c: [full(parts[c][:, at + r : at + r + 1]) for r in range(8)] for c in range(b + 1, count)}
        over = []
        for r in range(8):
            over.append(1.0 / cell[r][r])
            for s in range(r + 1, 8):
                ratio = cell[s][r] * over[r]
                for t in range(r + 1, s + 1):
                    cell[s][t] = cell[s][t] - ratio * cell[t][r]
                row[s] = row[s] - ratio * row[r]
                for values in column.values():
                    values[s] = values[s] - ratio * values[r]
        for c, values in column.items():
            for r in range(8):
                parts[c] = parts[c] - values[r] * (row[r] * over[r])
        own = row[0] / jnp.sqrt(cell[0][0])
        for s in range(1, 8):
            own = jnp.where(sub == s, row[s] / jnp.sqrt(cell[s][s]), own)
        done.append(own)
    return jnp.concatenate(done, axis=0)[:, k:]


def pack(gram):
    half = gram.shape[0] // 2
    return jnp.concatenate([gram[:half], gram[half:]], axis=1)


def unpack(packed):
    k = packed.shape[1] // 2
    return jnp.concatenate([packed[:, :k], packed[:, k:]], axis=0)


def kernel(
    n, m, total_rows,
    tiles_in, rows_in, columns_in, count_in, start_in, seeds_in,
    unit_out, centres_out,
    tiles, rows_ref, columns_ref, count_ref, seeds,
    matrix, basis0, basis1, images0, images1, gram_dev, gram_group,
    chooser, seed_group, right, left, square, units, weights, den, weights_scale, sums, final,
    in_sems, out_sems, *sems,
):
    me, g = lax.axis_index("dev"), lax.axis_index("group")
    pairs = [(sems[2 * i], sems[2 * i + 1]) for i in range(len(sems) // 2)]
    slots, block = tiles.shape[0], tiles.shape[1]
    width, local_rows = start_in.shape
    row_blocks = local_rows // block
    part = seeds.shape[1]

    barrier = pltpu.get_barrier_semaphore()
    for axis, size, index in (("dev", n, me), ("group", m, g)):
        loop(
            size - 1,
            lambda i: pl.semaphore_signal(
                barrier, inc=1, device_id={axis: lax.rem(index + 1 + i, size)}, device_id_type=MESH
            ),
        )
    loads = [(start_in.at[:, r * block : (r + 1) * block], basis0.at[me * row_blocks + r]) for r in range(row_blocks)]
    loads += [(rows_in, rows_ref), (columns_in, columns_ref), (count_in, count_ref), (seeds_in.at[me], seeds)]
    loads += [(tiles_in, tiles)]
    loads = [pltpu.make_async_copy(a, b, in_sems.at[i]) for i, (a, b) in enumerate(loads)]
    for load in loads:
        load.start()
    for load in loads:
        load.wait()
    pl.semaphore_wait(barrier, n - 1 + m - 1)

    used = iter(pairs)
    pending = []

    def exchange(axis, land, source=None):
        size, index = (n, me) if axis == "dev" else (m, g)
        made = Exchange(axis, size, index, land, next(used), source)
        made.start()
        pending.append(made)
        return made

    gather = exchange("dev", lambda d: basis0.at[pl.ds(d * row_blocks, row_blocks)])
    count = count_ref[0, 0]
    for s in range(slots):
        for r in range(row_blocks):
            keep = jnp.logical_and(rows_ref[s] == r, s < count)
            matrix[r * block : (r + 1) * block, s * block : (s + 1) * block] = tiles[s] * jnp.where(
                keep, 1.0, 0.0
            ).astype(jnp.bfloat16)

    def choose(d):
        first_row = (g * n + d) * local_rows
        chooser[d] = jnp.where(
            lax.broadcasted_iota(jnp.int32, (local_rows, part), 0) == seeds[...] - first_row, 1.0, 0.0
        ).astype(jnp.bfloat16)
        right[d, 3 * width :] = jnp.ones((MASS_ROWS, local_rows), jnp.bfloat16)
        left[d, 2 * width :] = jnp.ones((MASS_ROWS, local_rows), jnp.bfloat16)

    loop(n, choose)

    def apply(basis):
        picked = jnp.concatenate([basis[columns_ref[s]] for s in range(slots)], axis=1)
        return lax.dot_general(picked, matrix[...], NT, preferred_element_type=F32)

    def start_gram(image, turn):
        gram_dev[turn, me] = pack(mm(image, image, NT))
        return exchange("dev", lambda d, turn=turn: gram_dev.at[turn, d])

    def end_gram(first, turn):
        first.wait_recv()
        gram_group[turn, g] = fold(n, gram_dev.at[turn])
        return exchange("group", lambda d, turn=turn: gram_group.at[turn, d])

    gather.wait_recv()
    image = apply(basis0)
    first = start_gram(image, 0)
    images0[me] = image
    gather = exchange("dev", lambda d: images0.at[d])
    second = end_gram(first, 0)
    second.wait_recv()
    inverse = factor_inverse(unpack(fold(m, gram_group.at[0])))
    gather.wait_recv()

    def solve(d):
        solved = mm(inverse, images0[d])
        for r in range(row_blocks):
            basis1[d * row_blocks + r] = solved[:, r * block : (r + 1) * block].astype(jnp.bfloat16)

    loop(n, solve)
    image = apply(basis1)
    first = start_gram(image, 1)
    images1[me] = image
    gather = Gather(n, me, lambda d: images1.at[d], [next(used) for _ in range(2)])
    gather.start()
    second = end_gram(first, 1)
    gather.relay()
    gather.wait_recv()

    def chosen(d):
        pieces = dot16(jnp.concatenate(three(images1[d]), axis=0), chooser[d])
        return pieces[:width] + pieces[width : 2 * width] + pieces[2 * width :]

    seed_group[g] = total_of(n, chosen)
    seeding = exchange("group", lambda d: seed_group.at[d])
    second.wait_recv()
    inverse = factor_inverse(unpack(fold(m, gram_group.at[1])))

    def spread(mass):
        at = lax.broadcasted_iota(jnp.int32, (MASS_ROWS, part), 0)
        high, low = (v.astype(F32) for v in high_low(mass))
        return jnp.where(at == 0, high, jnp.where(at == 1, low, 0.0)).astype(jnp.bfloat16)

    def normalise(image_t):
        embedding = mm(inverse, image_t) * jnp.sqrt(F32(total_rows))
        return embedding / jnp.sqrt(jnp.sum(embedding * embedding, axis=0, keepdims=True) + 1e-06)

    def embed(d):
        unit = normalise(images1[d])
        units[d] = unit
        square[d] = -SHARPNESS * jnp.sum(unit * unit, axis=0, keepdims=True)
        high, low = high_low(unit)
        for at, piece in enumerate((high, low, high)):
            right[d, at * width : (at + 1) * width] = piece
        left[d, :width] = high
        left[d, width : 2 * width] = low

    loop(n, embed)
    unit_copy = pltpu.make_async_copy(units.at[me], unit_out, out_sems.at[0])
    unit_copy.start()
    seeding.wait_recv()
    centres = normalise(fold(m, seed_group))
    for turn in range(KSTEPS):
        high, low = high_low(2.0 * SHARPNESS * centres)
        bias = [v.astype(F32) for v in three(-SHARPNESS * jnp.sum(centres * centres, axis=0, keepdims=True))]
        bias = jnp.concatenate([*bias, jnp.zeros((MASS_ROWS - len(bias), part), F32)], axis=0).astype(jnp.bfloat16)
        table = jnp.concatenate([high, high, low, bias], axis=0)

        def weigh(d):
            values = jnp.exp(dot16(table, right[d], TN) + square[d])
            weights[d] = values
            den[turn, me, pl.ds(d, 1)] = jnp.sum(values, axis=0, keepdims=True)

        loop(n, weigh)
        exchange("dev", lambda d, turn=turn: den.at[turn, d]).wait_recv()
        units_of = 1.0 / fold(n, den.at[turn])
        weights_scale[...] = units_of

        def gathered(d):
            member = weights[d] * weights_scale[pl.ds(d, 1)]
            return dot16(left[d], member.astype(jnp.bfloat16), NT)

        pair = total_of(n, gathered)
        mass = pair[2 * width : 2 * width + 1]
        sums[turn, g, :width] = (pair[:width] + pair[width : 2 * width]).astype(jnp.bfloat16)
        sums[turn, g, width:] = spread(mass)
        exchange("group", lambda d, turn=turn: sums.at[turn, d]).wait_recv()
        total = fold(m, sums.at[turn])
        centres = total[:width] / (total[width : width + 1] + total[width + 1 : width + 2])
    final[...] = centres.astype(jnp.bfloat16)
    own_copy = pltpu.make_async_copy(final, centres_out.at[me], out_sems.at[1])
    own_copy.start()
    exchange("dev", lambda d: centres_out.at[d], lambda p: final).wait_recv()
    own_copy.wait()
    unit_copy.wait()
    for made in pending:
        made.wait_send()
    gather.wait_send()


def widen(n, unit_in, parts, unit_out, centres_out):
    unit_out[...] = unit_in[...]
    centres_out[...] = jnp.concatenate([parts[d].astype(F32) for d in range(n)], axis=1)


def local(tile_values, tile_rows, tile_columns, tile_count, start_basis, seed_rows):
    n, m = lax.axis_size("dev"), lax.axis_size("group")
    slots, block = tile_values.shape[0], tile_values.shape[1]
    local_rows, width = start_basis.shape
    row_blocks = local_rows // block
    clusters = seed_rows.shape[0]
    part = clusters // n
    vmem = pl.BlockSpec(memory_space=pltpu.VMEM)
    anywhere = pl.BlockSpec(memory_space=pl.ANY)
    half = (width // 2, 2 * width)
    B16 = jnp.bfloat16
    axes = ["dev", "dev", "dev", "group", "dev", "dev", "dev", "group", "group"]
    axes += ["dev", "group"] * KSTEPS + ["dev"]
    sems = []
    for axis in axes:
        sems += [pltpu.SemaphoreType.DMA((n if axis == "dev" else m,))] * 2
    unit, centres = pl.pallas_call(
        functools.partial(kernel, n, m, local_rows * n * m),
        out_shape=(
            pltpu.VMEM((width, local_rows), F32),
            pltpu.VMEM((n, width, part), B16),
        ),
        in_specs=[anywhere] * 6,
        out_specs=(vmem, vmem),
        scratch_shapes=[
            pltpu.VMEM(tile_values.shape, B16),
            pltpu.SMEM(tile_rows.shape, jnp.int32),
            pltpu.SMEM(tile_columns.shape, jnp.int32),
            pltpu.SMEM((1, 1), jnp.int32),
            pltpu.VMEM((1, part), jnp.int32),
            pltpu.VMEM((local_rows, slots * block), B16),
            pltpu.VMEM((n * row_blocks, width, block), B16),
            pltpu.VMEM((n * row_blocks, width, block), B16),
            pltpu.VMEM((n, width, local_rows), F32),
            pltpu.VMEM((n, width, local_rows), F32),
            pltpu.VMEM((2, n, *half), F32),
            pltpu.VMEM((2, m, *half), F32),
            pltpu.VMEM((n, local_rows, part), B16),
            pltpu.VMEM((m, width, part), F32),
            pltpu.VMEM((n, 3 * width + MASS_ROWS, local_rows), B16),
            pltpu.VMEM((n, 2 * width + MASS_ROWS, local_rows), B16),
            pltpu.VMEM((n, 1, local_rows), F32),
            pltpu.VMEM((n, width, local_rows), F32),
            pltpu.VMEM((n, part, local_rows), F32),
            pltpu.VMEM((KSTEPS, n, n, local_rows), F32),
            pltpu.VMEM((n, local_rows), F32),
            pltpu.VMEM((KSTEPS, m, width + MASS_ROWS, part), B16),
            pltpu.VMEM((width, part), B16),
            pltpu.SemaphoreType.DMA((row_blocks + 5,)),
            pltpu.SemaphoreType.DMA((2,)),
            *sems,
        ],
        compiler_params=pltpu.CompilerParams(
            collective_id=0, has_side_effects=True, vmem_limit_bytes=58 * 1024 * 1024
        ),
        name="spectral",
    )(tile_values, tile_rows, tile_columns, tile_count.reshape(1, 1), start_basis.T, seed_rows.reshape(n, 1, part))
    vmem = pl.BlockSpec(memory_space=pltpu.VMEM)
    unit, centres = pl.pallas_call(
        functools.partial(widen, n),
        out_shape=(
            jax.ShapeDtypeStruct((width, local_rows), F32),
            jax.ShapeDtypeStruct((width, clusters), F32),
        ),
        in_specs=[vmem, vmem],
        out_specs=(vmem, vmem),
        name="widen",
    )(pltpu.with_memory_space_constraint(unit, pltpu.VMEM), pltpu.with_memory_space_constraint(centres, pltpu.VMEM))
    return unit.T, centres.T


def solution(mesh):
    return jax.shard_map(
        local,
        mesh=mesh,
        in_specs=(
            P(("group", "dev"), None, None),
            P(("group", "dev")),
            P(("group", "dev")),
            P(("group", "dev")),
            P(("group", "dev"), None),
            P(),
        ),
        out_specs=(P(("group", "dev"), None), P()),
        check_vma=False,
    )
```

```python
import functools

import jax
import jax.numpy as jnp
from jax import lax
from jax.experimental import pallas as pl
from jax.experimental.pallas import tpu as pltpu
from jax.sharding import PartitionSpec as P

KSTEPS = 2
SHARPNESS = 4.0
MASS_ROWS = 16
LANES = 128
MESH = pl.DeviceIdType.MESH
F32 = jnp.float32
HIGHEST = lax.Precision.HIGHEST
NN = (((1,), (0,)), ((), ()))
NT = (((1,), (1,)), ((), ()))
TN = (((0,), (0,)), ((), ()))


def mm(a, b, dims=NN):
    return lax.dot_general(a, b, dims, precision=HIGHEST, preferred_element_type=F32)


def high_low(x):
    high = x.astype(jnp.bfloat16)
    return high, (x - high.astype(F32)).astype(jnp.bfloat16)


def dot16(a, b, dims=NN):
    return lax.dot_general(a, b, dims, preferred_element_type=F32)


def three(x):
    high = x.astype(jnp.bfloat16)
    return (high, *high_low(x - high.astype(F32)))


def loop(n, body):
    if n <= 8:
        for i in range(n):
            body(i)
    else:

        def step(i, carry):
            body(i)
            return carry

        lax.fori_loop(0, n, step, 0)


def fold(n, ref):
    total = ref[0].astype(F32)
    if n <= 8:
        for i in range(1, n):
            total = total + ref[i].astype(F32)
        return total
    return lax.fori_loop(1, n, lambda i, total: total + ref[i].astype(F32), total)


def small(n):
    return n <= 8 and n & (n - 1) == 0


def flip(me, mask):
    out, bit = me, 1
    while bit <= mask:
        if mask & bit:
            out = out + bit - 2 * bit * lax.rem(out // bit, 2)
        bit *= 2
    return out


class Exchange:
    def __init__(self, axis, n, me, land, sems, source=None):
        self.axis, self.n, self.me = axis, n, me
        self.land, self.source = land, source
        self.send, self.recv = sems

    def copy(self, peer, slot):
        source = self.land(self.me) if self.source is None else self.source(peer)
        return pltpu.make_async_remote_copy(
            src_ref=source,
            dst_ref=self.land(slot),
            send_sem=self.send.at[peer],
            recv_sem=self.recv.at[slot],
            device_id={self.axis: peer},
            device_id_type=MESH,
        )

    def peer(self, i):
        if small(self.n):
            return flip(self.me, self.n - 1 - i)
        return lax.rem(self.me + 1 + i, self.n)

    def start(self):
        loop(self.n - 1, lambda i: self.copy(self.peer(i), self.me).start())

    def wait_recv(self):
        loop(self.n - 1, lambda i: self.copy(self.peer(i), self.peer(i)).wait_recv())

    def wait_send(self):
        loop(self.n - 1, lambda i: self.copy(self.peer(i), self.me).wait_send())


def total_of(n, value):
    total = value(0)
    if n <= 8:
        for d in range(1, n):
            total = total + value(d)
        return total
    return lax.fori_loop(1, n, lambda d, total: total + value(d), total)


class Gather:
    def __init__(self, n, me, land, pairs):
        self.n, self.me, self.land = n, me, land
        self.pairs = pairs
        self.twin = self.me + 1 - 2 * lax.rem(self.me, 2)

    def copy(self, owner, slot, to, stage):
        send, recv = self.pairs[stage]
        return pltpu.make_async_remote_copy(
            src_ref=self.land(owner),
            dst_ref=self.land(owner),
            send_sem=send.at[slot],
            recv_sem=recv.at[owner],
            device_id={"dev": to},
            device_id_type=MESH,
        )

    def far(self, i):
        if small(self.n):
            return flip(self.me, 2 * (i + 1))
        return lax.rem(self.me + 2 + 2 * i, self.n)

    def start(self):
        self.copy(self.me, self.me, self.twin, 1).start()
        last = self.n // 2 - 2
        loop(last + 1, lambda i: self.copy(self.me, self.far(last - i), self.far(last - i), 0).start())

    def relay(self):
        def one(i):
            owner = self.far(i)
            self.copy(owner, owner, owner, 0).wait_recv()
            self.copy(owner, owner, self.twin, 1).start()

        loop(self.n // 2 - 1, one)

    def other(self, i):
        return lax.rem(self.twin + 2 * i, self.n)

    def wait_recv(self):
        loop(self.n // 2, lambda i: self.copy(self.other(i), self.other(i), self.twin, 1).wait_recv())

    def wait_send(self):
        self.copy(self.me, self.me, self.twin, 1).wait_send()

        def one(i):
            owner = self.far(i)
            self.copy(self.me, owner, owner, 0).wait_send()
            self.copy(owner, owner, self.twin, 1).wait_send()

        loop(self.n // 2 - 1, one)


def factor_inverse(gram):
    k = gram.shape[0]
    wide = 2 * k
    rows = lax.broadcasted_iota(jnp.int32, (k, k), 0)
    lanes = lax.broadcasted_iota(jnp.int32, (k, k), 1)
    table = jnp.concatenate([gram, jnp.where(rows == lanes, 1.0, 0.0).astype(F32)], axis=1)
    count = k // 8
    parts = [table[8 * b : 8 * b + 8] for b in range(count)]
    sub = lax.broadcasted_iota(jnp.int32, (8, wide), 0)

    def full(v):
        return jnp.broadcast_to(v, (8, wide))

    done = []
    for b in range(count):
        own, at = parts[b], 8 * b
        row = [full(own[s : s + 1]) for s in range(8)]
        cell = [[full(own[s : s + 1, at + r : at + r + 1]) for r in range(s + 1)] for s in range(8)]
        column = {c: [full(parts[c][:, at + r : at + r + 1]) for r in range(8)] for c in range(b + 1, count)}
        over = []
        for r in range(8):
            over.append(1.0 / cell[r][r])
            for s in range(r + 1, 8):
                ratio = cell[s][r] * over[r]
                for t in range(r + 1, s + 1):
                    cell[s][t] = cell[s][t] - ratio * cell[t][r]
                row[s] = row[s] - ratio * row[r]
                for values in column.values():
                    values[s] = values[s] - ratio * values[r]
        for c, values in column.items():
            for r in range(8):
                parts[c] = parts[c] - values[r] * (row[r] * over[r])
        own = row[0] / jnp.sqrt(cell[0][0])
        for s in range(1, 8):
            own = jnp.where(sub == s, row[s] / jnp.sqrt(cell[s][s]), own)
        done.append(own)
    return jnp.concatenate(done, axis=0)[:, k:]


def pack(gram):
    half = gram.shape[0] // 2
    return jnp.concatenate([gram[:half], gram[half:]], axis=1)


def unpack(packed):
    k = packed.shape[1] // 2
    return jnp.concatenate([packed[:, :k], packed[:, k:]], axis=0)


def kernel(
    n, m, total_rows,
    tiles_in, rows_in, columns_in, count_in, start_in, seeds_in,
    unit_out, centres_out,
    tiles, rows_ref, columns_ref, count_ref, seeds,
    matrix, basis0, basis1, images0, images1, gram_dev, gram_group,
    chooser, seed_group, right, left, square, units, weights, den, weights_scale, sums, final,
    in_sems, out_sems, *sems,
):
    me, g = lax.axis_index("dev"), lax.axis_index("group")
    pairs = [(sems[2 * i], sems[2 * i + 1]) for i in range(len(sems) // 2)]
    slots, block = tiles.shape[0], tiles.shape[1]
    width, local_rows = start_in.shape
    row_blocks = local_rows // block
    part = seeds.shape[1]

    barrier = pltpu.get_barrier_semaphore()
    for axis, size, index in (("dev", n, me), ("group", m, g)):
        loop(
            size - 1,
            lambda i: pl.semaphore_signal(
                barrier, inc=1, device_id={axis: lax.rem(index + 1 + i, size)}, device_id_type=MESH
            ),
        )
    loads = [(start_in.at[:, r * block : (r + 1) * block], basis0.at[me * row_blocks + r]) for r in range(row_blocks)]
    loads += [(rows_in, rows_ref), (columns_in, columns_ref), (count_in, count_ref), (seeds_in.at[me], seeds)]
    loads += [(tiles_in, tiles)]
    loads = [pltpu.make_async_copy(a, b, in_sems.at[i]) for i, (a, b) in enumerate(loads)]
    for load in loads:
        load.start()
    for load in loads:
        load.wait()
    pl.semaphore_wait(barrier, n - 1 + m - 1)

    used = iter(pairs)
    pending = []

    def exchange(axis, land, source=None):
        size, index = (n, me) if axis == "dev" else (m, g)
        made = Exchange(axis, size, index, land, next(used), source)
        made.start()
        pending.append(made)
        return made

    gather = exchange("dev", lambda d: basis0.at[pl.ds(d * row_blocks, row_blocks)])
    count = count_ref[0, 0]
    for s in range(slots):
        for r in range(row_blocks):
            keep = jnp.logical_and(rows_ref[s] == r, s < count)
            matrix[r * block : (r + 1) * block, s * block : (s + 1) * block] = tiles[s] * jnp.where(
                keep, 1.0, 0.0
            ).astype(jnp.bfloat16)

    def choose(d):
        first_row = (g * n + d) * local_rows
        chooser[d] = jnp.where(
            lax.broadcasted_iota(jnp.int32, (local_rows, part), 0) == seeds[...] - first_row, 1.0, 0.0
        ).astype(jnp.bfloat16)
        right[d, 3 * width :] = jnp.ones((MASS_ROWS, local_rows), jnp.bfloat16)
        left[d, 2 * width :] = jnp.ones((MASS_ROWS, local_rows), jnp.bfloat16)

    def apply(basis):
        picked = jnp.concatenate([basis[columns_ref[s]] for s in range(slots)], axis=1)
        return lax.dot_general(picked, matrix[...], NT, preferred_element_type=F32)

    def start_gram(image, turn):
        gram_dev[turn, me] = pack(mm(image, image, NT))
        return exchange("dev", lambda d, turn=turn: gram_dev.at[turn, d])

    def end_gram(first, turn):
        first.wait_recv()
        gram_group[turn, g] = fold(n, gram_dev.at[turn])
        return exchange("group", lambda d, turn=turn: gram_group.at[turn, d])

    loop(n, choose)
    gather.wait_recv()
    image = apply(basis0)
    first = start_gram(image, 0)
    images0[me] = image
    gather0 = Gather(n, me, lambda d: images0.at[d], [next(used) for _ in range(2)])
    gather0.start()
    second = end_gram(first, 0)
    gather0.relay()
    second.wait_recv()
    inverse = factor_inverse(unpack(fold(m, gram_group.at[0])))
    gather0.wait_recv()

    def solve(d):
        solved = mm(inverse, images0[d])
        for r in range(row_blocks):
            basis1[d * row_blocks + r] = solved[:, r * block : (r + 1) * block].astype(jnp.bfloat16)

    loop(n, solve)
    image = apply(basis1)
    first = start_gram(image, 1)
    images1[me] = image
    gather = Gather(n, me, lambda d: images1.at[d], [next(used) for _ in range(2)])
    gather.start()
    second = end_gram(first, 1)
    gather.relay()
    gather.wait_recv()

    def chosen(d):
        pieces = dot16(jnp.concatenate(three(images1[d]), axis=0), chooser[d])
        return pieces[:width] + pieces[width : 2 * width] + pieces[2 * width :]

    seed_group[g] = total_of(n, chosen)
    seeding = exchange("group", lambda d: seed_group.at[d])
    second.wait_recv()
    inverse = factor_inverse(unpack(fold(m, gram_group.at[1])))

    def spread(mass):
        at = lax.broadcasted_iota(jnp.int32, (MASS_ROWS, part), 0)
        high, low = (v.astype(F32) for v in high_low(mass))
        return jnp.where(at == 0, high, jnp.where(at == 1, low, 0.0)).astype(jnp.bfloat16)

    def normalise(image_t):
        embedding = mm(inverse, image_t) * jnp.sqrt(F32(total_rows))
        return embedding / jnp.sqrt(jnp.sum(embedding * embedding, axis=0, keepdims=True) + 1e-06)

    def embed(d):
        unit = normalise(images1[d])
        units[d] = unit
        square[d] = -SHARPNESS * jnp.sum(unit * unit, axis=0, keepdims=True)
        high, low = high_low(unit)
        for at, piece in enumerate((high, low, high)):
            right[d, at * width : (at + 1) * width] = piece
        left[d, :width] = high
        left[d, width : 2 * width] = low

    loop(n, embed)
    unit_copy = pltpu.make_async_copy(units.at[me], unit_out, out_sems.at[0])
    unit_copy.start()
    seeding.wait_recv()
    centres = normalise(fold(m, seed_group))
    for turn in range(KSTEPS):
        high, low = high_low(2.0 * SHARPNESS * centres)
        bias = [v.astype(F32) for v in three(-SHARPNESS * jnp.sum(centres * centres, axis=0, keepdims=True))]
        bias = jnp.concatenate([*bias, jnp.zeros((MASS_ROWS - len(bias), part), F32)], axis=0).astype(jnp.bfloat16)
        table = jnp.concatenate([high, high, low, bias], axis=0)

        def weigh(d):
            values = jnp.exp(dot16(table, right[d], TN) + square[d])
            weights[d] = values
            den[turn, me, pl.ds(d, 1)] = jnp.sum(values, axis=0, keepdims=True)

        loop(n, weigh)
        exchange("dev", lambda d, turn=turn: den.at[turn, d]).wait_recv()
        units_of = 1.0 / fold(n, den.at[turn])
        weights_scale[...] = units_of

        def gathered(d):
            member = weights[d] * weights_scale[pl.ds(d, 1)]
            return dot16(left[d], member.astype(jnp.bfloat16), NT)

        pair = total_of(n, gathered)
        mass = pair[2 * width : 2 * width + 1]
        sums[turn, g, :width] = (pair[:width] + pair[width : 2 * width]).astype(jnp.bfloat16)
        sums[turn, g, width:] = spread(mass)
        exchange("group", lambda d, turn=turn: sums.at[turn, d]).wait_recv()
        total = fold(m, sums.at[turn])
        centres = total[:width] / (total[width : width + 1] + total[width + 1 : width + 2])
    final[...] = centres.astype(jnp.bfloat16)
    own_copy = pltpu.make_async_copy(final, centres_out.at[me], out_sems.at[1])
    own_copy.start()
    exchange("dev", lambda d: centres_out.at[d], lambda p: final).wait_recv()
    own_copy.wait()
    unit_copy.wait()
    for made in pending:
        made.wait_send()
    gather0.wait_send()
    gather.wait_send()


def widen(n, unit_in, parts, unit_out, centres_out):
    unit_out[...] = unit_in[...]
    centres_out[...] = jnp.concatenate([parts[d].astype(F32) for d in range(n)], axis=1)


def local(tile_values, tile_rows, tile_columns, tile_count, start_basis, seed_rows):
    n, m = lax.axis_size("dev"), lax.axis_size("group")
    slots, block = tile_values.shape[0], tile_values.shape[1]
    local_rows, width = start_basis.shape
    row_blocks = local_rows // block
    clusters = seed_rows.shape[0]
    part = clusters // n
    vmem = pl.BlockSpec(memory_space=pltpu.VMEM)
    anywhere = pl.BlockSpec(memory_space=pl.ANY)
    half = (width // 2, 2 * width)
    B16 = jnp.bfloat16
    axes = ["dev", "dev", "dev", "dev", "group", "dev", "dev", "dev", "group", "group"]
    axes += ["dev", "group"] * KSTEPS + ["dev"]
    sems = []
    for axis in axes:
        sems += [pltpu.SemaphoreType.DMA((n if axis == "dev" else m,))] * 2
    unit, centres = pl.pallas_call(
        functools.partial(kernel, n, m, local_rows * n * m),
        out_shape=(
            pltpu.VMEM((width, local_rows), F32),
            pltpu.VMEM((n, width, part), B16),
        ),
        in_specs=[anywhere] * 6,
        out_specs=(vmem, vmem),
        scratch_shapes=[
            pltpu.VMEM(tile_values.shape, B16),
            pltpu.SMEM(tile_rows.shape, jnp.int32),
            pltpu.SMEM(tile_columns.shape, jnp.int32),
            pltpu.SMEM((1, 1), jnp.int32),
            pltpu.VMEM((1, part), jnp.int32),
            pltpu.VMEM((local_rows, slots * block), B16),
            pltpu.VMEM((n * row_blocks, width, block), B16),
            pltpu.VMEM((n * row_blocks, width, block), B16),
            pltpu.VMEM((n, width, local_rows), F32),
            pltpu.VMEM((n, width, local_rows), F32),
            pltpu.VMEM((2, n, *half), F32),
            pltpu.VMEM((2, m, *half), F32),
            pltpu.VMEM((n, local_rows, part), B16),
            pltpu.VMEM((m, width, part), F32),
            pltpu.VMEM((n, 3 * width + MASS_ROWS, local_rows), B16),
            pltpu.VMEM((n, 2 * width + MASS_ROWS, local_rows), B16),
            pltpu.VMEM((n, 1, local_rows), F32),
            pltpu.VMEM((n, width, local_rows), F32),
            pltpu.VMEM((n, part, local_rows), F32),
            pltpu.VMEM((KSTEPS, n, n, local_rows), F32),
            pltpu.VMEM((n, local_rows), F32),
            pltpu.VMEM((KSTEPS, m, width + MASS_ROWS, part), B16),
            pltpu.VMEM((width, part), B16),
            pltpu.SemaphoreType.DMA((row_blocks + 5,)),
            pltpu.SemaphoreType.DMA((2,)),
            *sems,
        ],
        compiler_params=pltpu.CompilerParams(
            collective_id=0, has_side_effects=True, vmem_limit_bytes=58 * 1024 * 1024
        ),
        name="spectral",
    )(tile_values, tile_rows, tile_columns, tile_count.reshape(1, 1), start_basis.T, seed_rows.reshape(n, 1, part))
    vmem = pl.BlockSpec(memory_space=pltpu.VMEM)
    unit, centres = pl.pallas_call(
        functools.partial(widen, n),
        out_shape=(
            jax.ShapeDtypeStruct((width, local_rows), F32),
            jax.ShapeDtypeStruct((width, clusters), F32),
        ),
        in_specs=[vmem, vmem],
        out_specs=(vmem, vmem),
        name="widen",
    )(pltpu.with_memory_space_constraint(unit, pltpu.VMEM), pltpu.with_memory_space_constraint(centres, pltpu.VMEM))
    return unit.T, centres.T


def solution(mesh):
    return jax.shard_map(
        local,
        mesh=mesh,
        in_specs=(
            P(("group", "dev"), None, None),
            P(("group", "dev")),
            P(("group", "dev")),
            P(("group", "dev")),
            P(("group", "dev"), None),
            P(),
        ),
        out_specs=(P(("group", "dev"), None), P()),
        check_vma=False,
    )
```

```python
import functools

import jax
import jax.numpy as jnp
from jax import lax
from jax.experimental import pallas as pl
from jax.experimental.pallas import tpu as pltpu
from jax.sharding import PartitionSpec as P

KSTEPS = 2
SHARPNESS = 4.0
MASS_ROWS = 16
LANES = 128
MESH = pl.DeviceIdType.MESH
F32 = jnp.float32
HIGHEST = lax.Precision.HIGHEST
NN = (((1,), (0,)), ((), ()))
NT = (((1,), (1,)), ((), ()))
TN = (((0,), (0,)), ((), ()))


def mm(a, b, dims=NN):
    return lax.dot_general(a, b, dims, precision=HIGHEST, preferred_element_type=F32)


def high_low(x):
    high = x.astype(jnp.bfloat16)
    return high, (x - high.astype(F32)).astype(jnp.bfloat16)


def dot16(a, b, dims=NN):
    return lax.dot_general(a, b, dims, preferred_element_type=F32)


def three(x):
    high = x.astype(jnp.bfloat16)
    return (high, *high_low(x - high.astype(F32)))


def loop(n, body):
    if n <= 8:
        for i in range(n):
            body(i)
    else:

        def step(i, carry):
            body(i)
            return carry

        lax.fori_loop(0, n, step, 0)


def fold(n, ref):
    total = ref[0].astype(F32)
    if n <= 8:
        for i in range(1, n):
            total = total + ref[i].astype(F32)
        return total
    return lax.fori_loop(1, n, lambda i, total: total + ref[i].astype(F32), total)


def small(n):
    return n <= 8 and n & (n - 1) == 0


def flip(me, mask):
    out, bit = me, 1
    while bit <= mask:
        if mask & bit:
            out = out + bit - 2 * bit * lax.rem(out // bit, 2)
        bit *= 2
    return out


class Exchange:
    def __init__(self, axis, n, me, land, sems, source=None):
        self.axis, self.n, self.me = axis, n, me
        self.land, self.source = land, source
        self.send, self.recv = sems

    def copy(self, peer, slot):
        source = self.land(self.me) if self.source is None else self.source(peer)
        return pltpu.make_async_remote_copy(
            src_ref=source,
            dst_ref=self.land(slot),
            send_sem=self.send.at[peer],
            recv_sem=self.recv.at[slot],
            device_id={self.axis: peer},
            device_id_type=MESH,
        )

    def peer(self, i):
        if small(self.n):
            return flip(self.me, self.n - 1 - i)
        return lax.rem(self.me + 1 + i, self.n)

    def start(self):
        loop(self.n - 1, lambda i: self.copy(self.peer(i), self.me).start())

    def wait_recv(self):
        loop(self.n - 1, lambda i: self.copy(self.peer(i), self.peer(i)).wait_recv())

    def wait_send(self):
        loop(self.n - 1, lambda i: self.copy(self.peer(i), self.me).wait_send())


def total_of(n, value):
    total = value(0)
    if n <= 8:
        for d in range(1, n):
            total = total + value(d)
        return total
    return lax.fori_loop(1, n, lambda d, total: total + value(d), total)


class Gather:
    def __init__(self, n, me, land, pairs):
        self.n, self.me, self.land = n, me, land
        self.pairs = pairs
        self.twin = self.me + 1 - 2 * lax.rem(self.me, 2)

    def copy(self, owner, slot, to, stage):
        send, recv = self.pairs[stage]
        return pltpu.make_async_remote_copy(
            src_ref=self.land(owner),
            dst_ref=self.land(owner),
            send_sem=send.at[slot],
            recv_sem=recv.at[owner],
            device_id={"dev": to},
            device_id_type=MESH,
        )

    def far(self, i):
        if small(self.n):
            return flip(self.me, 2 * (i + 1))
        return lax.rem(self.me + 2 + 2 * i, self.n)

    def start(self):
        self.copy(self.me, self.me, self.twin, 1).start()
        last = self.n // 2 - 2
        loop(last + 1, lambda i: self.copy(self.me, self.far(last - i), self.far(last - i), 0).start())

    def relay(self):
        def one(i):
            owner = self.far(i)
            self.copy(owner, owner, owner, 0).wait_recv()
            self.copy(owner, owner, self.twin, 1).start()

        loop(self.n // 2 - 1, one)

    def other(self, i):
        return lax.rem(self.twin + 2 * i, self.n)

    def wait_recv(self):
        loop(self.n // 2, lambda i: self.copy(self.other(i), self.other(i), self.twin, 1).wait_recv())

    def wait_send(self):
        self.copy(self.me, self.me, self.twin, 1).wait_send()

        def one(i):
            owner = self.far(i)
            self.copy(self.me, owner, owner, 0).wait_send()
            self.copy(owner, owner, self.twin, 1).wait_send()

        loop(self.n // 2 - 1, one)


def factor_inverse(gram):
    k = gram.shape[0]
    wide = 2 * k
    rows = lax.broadcasted_iota(jnp.int32, (k, k), 0)
    lanes = lax.broadcasted_iota(jnp.int32, (k, k), 1)
    table = jnp.concatenate([gram, jnp.where(rows == lanes, 1.0, 0.0).astype(F32)], axis=1)
    count = k // 8
    parts = [table[8 * b : 8 * b + 8] for b in range(count)]
    sub = lax.broadcasted_iota(jnp.int32, (8, wide), 0)

    def full(v):
        return jnp.broadcast_to(v, (8, wide))

    done = []
    for b in range(count):
        own, at = parts[b], 8 * b
        row = [full(own[s : s + 1]) for s in range(8)]
        cell = [[full(own[s : s + 1, at + r : at + r + 1]) for r in range(s + 1)] for s in range(8)]
        column = {c: [full(parts[c][:, at + r : at + r + 1]) for r in range(8)] for c in range(b + 1, count)}
        over = []
        for r in range(8):
            over.append(1.0 / cell[r][r])
            for s in range(r + 1, 8):
                ratio = cell[s][r] * over[r]
                for t in range(r + 1, s + 1):
                    cell[s][t] = cell[s][t] - ratio * cell[t][r]
                row[s] = row[s] - ratio * row[r]
                for values in column.values():
                    values[s] = values[s] - ratio * values[r]
        for c, values in column.items():
            for r in range(8):
                parts[c] = parts[c] - values[r] * (row[r] * over[r])
        own = row[0] / jnp.sqrt(cell[0][0])
        for s in range(1, 8):
            own = jnp.where(sub == s, row[s] / jnp.sqrt(cell[s][s]), own)
        done.append(own)
    return jnp.concatenate(done, axis=0)[:, k:]


def pack(gram):
    half = gram.shape[0] // 2
    return jnp.concatenate([gram[:half], gram[half:]], axis=1)


def unpack(packed):
    k = packed.shape[1] // 2
    return jnp.concatenate([packed[:, :k], packed[:, k:]], axis=0)


def kernel(
    n, m, total_rows,
    tiles_in, rows_in, columns_in, count_in, start_in, seeds_in,
    unit_out, centres_out,
    tiles, rows_ref, columns_ref, count_ref, seeds,
    matrix, basis0, basis1, images0, images1, gram_dev, gram_group,
    chooser, seed_group, right, left, square, units, weights, den, weights_scale, sums, final,
    in_sems, out_sems, *sems,
):
    me, g = lax.axis_index("dev"), lax.axis_index("group")
    pairs = [(sems[2 * i], sems[2 * i + 1]) for i in range(len(sems) // 2)]
    slots, block = tiles.shape[0], tiles.shape[1]
    width, local_rows = start_in.shape
    row_blocks = local_rows // block
    part = seeds.shape[1]

    barrier = pltpu.get_barrier_semaphore()
    for axis, size, index in (("dev", n, me), ("group", m, g)):
        loop(
            size - 1,
            lambda i: pl.semaphore_signal(
                barrier, inc=1, device_id={axis: lax.rem(index + 1 + i, size)}, device_id_type=MESH
            ),
        )
    loads = [(start_in.at[:, r * block : (r + 1) * block], basis0.at[me * row_blocks + r]) for r in range(row_blocks)]
    loads += [(rows_in, rows_ref), (columns_in, columns_ref), (count_in, count_ref), (seeds_in.at[me], seeds)]
    loads += [(tiles_in, tiles)]
    loads = [pltpu.make_async_copy(a, b, in_sems.at[i]) for i, (a, b) in enumerate(loads)]
    for load in loads:
        load.start()
    for load in loads:
        load.wait()
    pl.semaphore_wait(barrier, n - 1 + m - 1)

    used = iter(pairs)
    pending = []

    def exchange(axis, land, source=None):
        size, index = (n, me) if axis == "dev" else (m, g)
        made = Exchange(axis, size, index, land, next(used), source)
        made.start()
        pending.append(made)
        return made

    gather = exchange("dev", lambda d: basis0.at[pl.ds(d * row_blocks, row_blocks)])
    count = count_ref[0, 0]
    for s in range(slots):
        turned = tiles[s].T
        for r in range(row_blocks):
            keep = jnp.logical_and(rows_ref[s] == r, s < count)
            matrix[s * block : (s + 1) * block, r * block : (r + 1) * block] = turned * jnp.where(
                keep, 1.0, 0.0
            ).astype(jnp.bfloat16)

    def choose(d):
        first_row = (g * n + d) * local_rows
        chooser[d] = jnp.where(
            lax.broadcasted_iota(jnp.int32, (local_rows, part), 0) == seeds[...] - first_row, 1.0, 0.0
        ).astype(jnp.bfloat16)
        right[d, 3 * width :] = jnp.ones((MASS_ROWS, local_rows), jnp.bfloat16)
        left[d, 2 * width :] = jnp.ones((MASS_ROWS, local_rows), jnp.bfloat16)

    def apply(basis):
        picked = jnp.concatenate([basis[columns_ref[s]] for s in range(slots)], axis=1)
        return dot16(picked, matrix[...])

    def start_gram(image, turn):
        gram_dev[turn, me] = pack(mm(image, image, NT))
        return exchange("dev", lambda d, turn=turn: gram_dev.at[turn, d])

    def end_gram(first, turn):
        first.wait_recv()
        gram_group[turn, g] = fold(n, gram_dev.at[turn])
        return exchange("group", lambda d, turn=turn: gram_group.at[turn, d])

    loop(n, choose)
    gather.wait_recv()
    image = apply(basis0)
    first = start_gram(image, 0)
    images0[me] = image
    gather0 = Gather(n, me, lambda d: images0.at[d], [next(used) for _ in range(2)])
    gather0.start()
    second = end_gram(first, 0)
    gather0.relay()
    second.wait_recv()
    inverse = factor_inverse(unpack(fold(m, gram_group.at[0])))
    gather0.wait_recv()

    def solve(d):
        solved = mm(inverse, images0[d])
        for r in range(row_blocks):
            basis1[d * row_blocks + r] = solved[:, r * block : (r + 1) * block].astype(jnp.bfloat16)

    loop(n, solve)
    image = apply(basis1)
    first = start_gram(image, 1)
    images1[me] = image
    gather = Gather(n, me, lambda d: images1.at[d], [next(used) for _ in range(2)])
    gather.start()
    second = end_gram(first, 1)
    gather.relay()
    gather.wait_recv()

    def chosen(d):
        pieces = dot16(jnp.concatenate(three(images1[d]), axis=0), chooser[d])
        return pieces[:width] + pieces[width : 2 * width] + pieces[2 * width :]

    seed_group[g] = total_of(n, chosen)
    seeding = exchange("group", lambda d: seed_group.at[d])
    second.wait_recv()
    inverse = factor_inverse(unpack(fold(m, gram_group.at[1])))

    def spread(mass):
        at = lax.broadcasted_iota(jnp.int32, (MASS_ROWS, part), 0)
        high, low = (v.astype(F32) for v in high_low(mass))
        return jnp.where(at == 0, high, jnp.where(at == 1, low, 0.0)).astype(jnp.bfloat16)

    def normalise(image_t):
        embedding = mm(inverse, image_t) * jnp.sqrt(F32(total_rows))
        return embedding / jnp.sqrt(jnp.sum(embedding * embedding, axis=0, keepdims=True) + 1e-06)

    def embed(d):
        unit = normalise(images1[d])
        units[d] = unit
        square[d] = -SHARPNESS * jnp.sum(unit * unit, axis=0, keepdims=True)
        high, low = high_low(unit)
        for at, piece in enumerate((high, low, high)):
            right[d, at * width : (at + 1) * width] = piece
        left[d, :width] = high
        left[d, width : 2 * width] = low

    loop(n, embed)
    unit_copy = pltpu.make_async_copy(units.at[me], unit_out, out_sems.at[0])
    unit_copy.start()
    seeding.wait_recv()
    centres = normalise(fold(m, seed_group))
    for turn in range(KSTEPS):
        high, low = high_low(2.0 * SHARPNESS * centres)
        bias = [v.astype(F32) for v in three(-SHARPNESS * jnp.sum(centres * centres, axis=0, keepdims=True))]
        bias = jnp.concatenate([*bias, jnp.zeros((MASS_ROWS - len(bias), part), F32)], axis=0).astype(jnp.bfloat16)
        table = jnp.concatenate([high, high, low, bias], axis=0)

        def weigh(d):
            values = jnp.exp(dot16(table, right[d], TN) + square[d])
            weights[d] = values
            den[turn, me, pl.ds(d, 1)] = jnp.sum(values, axis=0, keepdims=True)

        loop(n, weigh)
        exchange("dev", lambda d, turn=turn: den.at[turn, d]).wait_recv()
        units_of = 1.0 / fold(n, den.at[turn])
        weights_scale[...] = units_of

        def gathered(d):
            member = weights[d] * weights_scale[pl.ds(d, 1)]
            return dot16(left[d], member.astype(jnp.bfloat16), NT)

        pair = total_of(n, gathered)
        mass = pair[2 * width : 2 * width + 1]
        sums[turn, g, :width] = (pair[:width] + pair[width : 2 * width]).astype(jnp.bfloat16)
        sums[turn, g, width:] = spread(mass)
        exchange("group", lambda d, turn=turn: sums.at[turn, d]).wait_recv()
        total = fold(m, sums.at[turn])
        centres = total[:width] / (total[width : width + 1] + total[width + 1 : width + 2])
    final[...] = centres.astype(jnp.bfloat16)
    own_copy = pltpu.make_async_copy(final, centres_out.at[me], out_sems.at[1])
    own_copy.start()
    exchange("dev", lambda d: centres_out.at[d], lambda p: final).wait_recv()
    own_copy.wait()
    unit_copy.wait()
    for made in pending:
        made.wait_send()
    gather0.wait_send()
    gather.wait_send()


def widen(n, unit_in, parts, unit_out, centres_out):
    unit_out[...] = unit_in[...]
    centres_out[...] = jnp.concatenate([parts[d].astype(F32) for d in range(n)], axis=1)


def local(tile_values, tile_rows, tile_columns, tile_count, start_basis, seed_rows):
    n, m = lax.axis_size("dev"), lax.axis_size("group")
    slots, block = tile_values.shape[0], tile_values.shape[1]
    local_rows, width = start_basis.shape
    row_blocks = local_rows // block
    clusters = seed_rows.shape[0]
    part = clusters // n
    vmem = pl.BlockSpec(memory_space=pltpu.VMEM)
    anywhere = pl.BlockSpec(memory_space=pl.ANY)
    half = (width // 2, 2 * width)
    B16 = jnp.bfloat16
    axes = ["dev", "dev", "dev", "dev", "group", "dev", "dev", "dev", "group", "group"]
    axes += ["dev", "group"] * KSTEPS + ["dev"]
    sems = []
    for axis in axes:
        sems += [pltpu.SemaphoreType.DMA((n if axis == "dev" else m,))] * 2
    unit, centres = pl.pallas_call(
        functools.partial(kernel, n, m, local_rows * n * m),
        out_shape=(
            pltpu.VMEM((width, local_rows), F32),
            pltpu.VMEM((n, width, part), B16),
        ),
        in_specs=[anywhere] * 6,
        out_specs=(vmem, vmem),
        scratch_shapes=[
            pltpu.VMEM(tile_values.shape, B16),
            pltpu.SMEM(tile_rows.shape, jnp.int32),
            pltpu.SMEM(tile_columns.shape, jnp.int32),
            pltpu.SMEM((1, 1), jnp.int32),
            pltpu.VMEM((1, part), jnp.int32),
            pltpu.VMEM((slots * block, local_rows), B16),
            pltpu.VMEM((n * row_blocks, width, block), B16),
            pltpu.VMEM((n * row_blocks, width, block), B16),
            pltpu.VMEM((n, width, local_rows), F32),
            pltpu.VMEM((n, width, local_rows), F32),
            pltpu.VMEM((2, n, *half), F32),
            pltpu.VMEM((2, m, *half), F32),
            pltpu.VMEM((n, local_rows, part), B16),
            pltpu.VMEM((m, width, part), F32),
            pltpu.VMEM((n, 3 * width + MASS_ROWS, local_rows), B16),
            pltpu.VMEM((n, 2 * width + MASS_ROWS, local_rows), B16),
            pltpu.VMEM((n, 1, local_rows), F32),
            pltpu.VMEM((n, width, local_rows), F32),
            pltpu.VMEM((n, part, local_rows), F32),
            pltpu.VMEM((KSTEPS, n, n, local_rows), F32),
            pltpu.VMEM((n, local_rows), F32),
            pltpu.VMEM((KSTEPS, m, width + MASS_ROWS, part), B16),
            pltpu.VMEM((width, part), B16),
            pltpu.SemaphoreType.DMA((row_blocks + 5,)),
            pltpu.SemaphoreType.DMA((2,)),
            *sems,
        ],
        compiler_params=pltpu.CompilerParams(
            collective_id=0, has_side_effects=True, vmem_limit_bytes=58 * 1024 * 1024
        ),
        name="spectral",
    )(tile_values, tile_rows, tile_columns, tile_count.reshape(1, 1), start_basis.T, seed_rows.reshape(n, 1, part))
    vmem = pl.BlockSpec(memory_space=pltpu.VMEM)
    unit, centres = pl.pallas_call(
        functools.partial(widen, n),
        out_shape=(
            jax.ShapeDtypeStruct((width, local_rows), F32),
            jax.ShapeDtypeStruct((width, clusters), F32),
        ),
        in_specs=[vmem, vmem],
        out_specs=(vmem, vmem),
        name="widen",
    )(pltpu.with_memory_space_constraint(unit, pltpu.VMEM), pltpu.with_memory_space_constraint(centres, pltpu.VMEM))
    return unit.T, centres.T


def solution(mesh):
    return jax.shard_map(
        local,
        mesh=mesh,
        in_specs=(
            P(("group", "dev"), None, None),
            P(("group", "dev")),
            P(("group", "dev")),
            P(("group", "dev")),
            P(("group", "dev"), None),
            P(),
        ),
        out_specs=(P(("group", "dev"), None), P()),
        check_vma=False,
    )
```

```python
import functools

import jax
import jax.numpy as jnp
from jax import lax
from jax.experimental import pallas as pl
from jax.experimental.pallas import tpu as pltpu
from jax.sharding import PartitionSpec as P

KSTEPS = 2
SHARPNESS = 4.0
MASS_ROWS = 16
LANES = 128
MESH = pl.DeviceIdType.MESH
F32 = jnp.float32
HIGHEST = lax.Precision.HIGHEST
NN = (((1,), (0,)), ((), ()))
NT = (((1,), (1,)), ((), ()))
TN = (((0,), (0,)), ((), ()))


def mm(a, b, dims=NN):
    return lax.dot_general(a, b, dims, precision=HIGHEST, preferred_element_type=F32)


def high_low(x):
    high = x.astype(jnp.bfloat16)
    return high, (x - high.astype(F32)).astype(jnp.bfloat16)


def dot16(a, b, dims=NN):
    return lax.dot_general(a, b, dims, preferred_element_type=F32)


def three(x):
    high = x.astype(jnp.bfloat16)
    return (high, *high_low(x - high.astype(F32)))


def loop(n, body):
    if n <= 8:
        for i in range(n):
            body(i)
    else:

        def step(i, carry):
            body(i)
            return carry

        lax.fori_loop(0, n, step, 0)


def fold(n, ref):
    total = ref[0].astype(F32)
    if n <= 8:
        for i in range(1, n):
            total = total + ref[i].astype(F32)
        return total
    return lax.fori_loop(1, n, lambda i, total: total + ref[i].astype(F32), total)


def small(n):
    return n <= 8 and n & (n - 1) == 0


def flip(me, mask):
    out, bit = me, 1
    while bit <= mask:
        if mask & bit:
            out = out + bit - 2 * bit * lax.rem(out // bit, 2)
        bit *= 2
    return out


class Exchange:
    def __init__(self, axis, n, me, land, sems, source=None):
        self.axis, self.n, self.me = axis, n, me
        self.land, self.source = land, source
        self.send, self.recv = sems

    def copy(self, peer, slot):
        source = self.land(self.me) if self.source is None else self.source(peer)
        return pltpu.make_async_remote_copy(
            src_ref=source,
            dst_ref=self.land(slot),
            send_sem=self.send.at[peer],
            recv_sem=self.recv.at[slot],
            device_id={self.axis: peer},
            device_id_type=MESH,
        )

    def peer(self, i):
        if small(self.n):
            return flip(self.me, self.n - 1 - i)
        return lax.rem(self.me + 1 + i, self.n)

    def start(self):
        loop(self.n - 1, lambda i: self.copy(self.peer(i), self.me).start())

    def wait_recv(self):
        loop(self.n - 1, lambda i: self.copy(self.peer(i), self.peer(i)).wait_recv())

    def wait_send(self):
        loop(self.n - 1, lambda i: self.copy(self.peer(i), self.me).wait_send())


def total_of(n, value):
    total = value(0)
    if n <= 8:
        for d in range(1, n):
            total = total + value(d)
        return total
    return lax.fori_loop(1, n, lambda d, total: total + value(d), total)


class Gather:
    def __init__(self, n, me, land, pairs):
        self.n, self.me, self.land = n, me, land
        self.pairs = pairs
        self.twin = self.me + 1 - 2 * lax.rem(self.me, 2)

    def copy(self, owner, slot, to, stage):
        send, recv = self.pairs[stage]
        return pltpu.make_async_remote_copy(
            src_ref=self.land(owner),
            dst_ref=self.land(owner),
            send_sem=send.at[slot],
            recv_sem=recv.at[owner],
            device_id={"dev": to},
            device_id_type=MESH,
        )

    def far(self, i):
        if small(self.n):
            return flip(self.me, 2 * (i + 1))
        return lax.rem(self.me + 2 + 2 * i, self.n)

    def start(self):
        self.copy(self.me, self.me, self.twin, 1).start()
        last = self.n // 2 - 2
        loop(last + 1, lambda i: self.copy(self.me, self.far(last - i), self.far(last - i), 0).start())

    def relay(self):
        def one(i):
            owner = self.far(i)
            self.copy(owner, owner, owner, 0).wait_recv()
            self.copy(owner, owner, self.twin, 1).start()

        loop(self.n // 2 - 1, one)

    def other(self, i):
        return lax.rem(self.twin + 2 * i, self.n)

    def wait_recv(self):
        loop(self.n // 2, lambda i: self.copy(self.other(i), self.other(i), self.twin, 1).wait_recv())

    def wait_send(self):
        self.copy(self.me, self.me, self.twin, 1).wait_send()

        def one(i):
            owner = self.far(i)
            self.copy(self.me, owner, owner, 0).wait_send()
            self.copy(owner, owner, self.twin, 1).wait_send()

        loop(self.n // 2 - 1, one)


def factor_inverse(gram):
    k = gram.shape[0]
    wide = 2 * k
    rows = lax.broadcasted_iota(jnp.int32, (k, k), 0)
    lanes = lax.broadcasted_iota(jnp.int32, (k, k), 1)
    table = jnp.concatenate([gram, jnp.where(rows == lanes, 1.0, 0.0).astype(F32)], axis=1)
    count = k // 8
    parts = [table[8 * b : 8 * b + 8] for b in range(count)]
    sub = lax.broadcasted_iota(jnp.int32, (8, wide), 0)

    def full(v):
        return jnp.broadcast_to(v, (8, wide))

    done = []
    for b in range(count):
        own, at = parts[b], 8 * b
        row = [full(own[s : s + 1]) for s in range(8)]
        cell = [[full(own[s : s + 1, at + r : at + r + 1]) for r in range(s + 1)] for s in range(8)]
        column = {c: [full(parts[c][:, at + r : at + r + 1]) for r in range(8)] for c in range(b + 1, count)}
        over = []
        for r in range(8):
            over.append(1.0 / cell[r][r])
            for s in range(r + 1, 8):
                ratio = cell[s][r] * over[r]
                for t in range(r + 1, s + 1):
                    cell[s][t] = cell[s][t] - ratio * cell[t][r]
                row[s] = row[s] - ratio * row[r]
                for values in column.values():
                    values[s] = values[s] - ratio * values[r]
        for c, values in column.items():
            for r in range(8):
                parts[c] = parts[c] - values[r] * (row[r] * over[r])
        own = row[0] / jnp.sqrt(cell[0][0])
        for s in range(1, 8):
            own = jnp.where(sub == s, row[s] / jnp.sqrt(cell[s][s]), own)
        done.append(own)
    return jnp.concatenate(done, axis=0)[:, k:]


def pack(gram):
    half = gram.shape[0] // 2
    return jnp.concatenate([gram[:half], gram[half:]], axis=1)


def unpack(packed):
    k = packed.shape[1] // 2
    return jnp.concatenate([packed[:, :k], packed[:, k:]], axis=0)


def kernel(
    n, m, total_rows,
    tiles_in, rows_in, columns_in, count_in, start_in, seeds_in,
    unit_out, centres_out,
    tiles, rows_ref, columns_ref, count_ref, seeds,
    matrix, basis0, basis1, images0, images1, gram_dev, gram_group,
    chooser, seed_group, right, left, square, units, weights, den, weights_scale, sums, final,
    in_sems, out_sems, *sems,
):
    me, g = lax.axis_index("dev"), lax.axis_index("group")
    pairs = [(sems[2 * i], sems[2 * i + 1]) for i in range(len(sems) // 2)]
    slots, block = tiles.shape[0], tiles.shape[1]
    width, local_rows = start_in.shape
    row_blocks = local_rows // block
    part = seeds.shape[1]

    barrier = pltpu.get_barrier_semaphore()
    for axis, size, index in (("dev", n, me), ("group", m, g)):
        loop(
            size - 1,
            lambda i: pl.semaphore_signal(
                barrier, inc=1, device_id={axis: lax.rem(index + 1 + i, size)}, device_id_type=MESH
            ),
        )
    loads = [(start_in.at[:, r * block : (r + 1) * block], basis0.at[me * row_blocks + r]) for r in range(row_blocks)]
    loads += [(rows_in, rows_ref), (columns_in, columns_ref), (count_in, count_ref), (seeds_in.at[me], seeds)]
    loads += [(tiles_in, tiles)]
    loads = [pltpu.make_async_copy(a, b, in_sems.at[i]) for i, (a, b) in enumerate(loads)]
    for load in loads:
        load.start()
    for load in loads:
        load.wait()
    pl.semaphore_wait(barrier, n - 1 + m - 1)

    used = iter(pairs)
    pending = []

    def exchange(axis, land, source=None):
        size, index = (n, me) if axis == "dev" else (m, g)
        made = Exchange(axis, size, index, land, next(used), source)
        made.start()
        pending.append(made)
        return made

    gather = exchange("dev", lambda d: basis0.at[pl.ds(d * row_blocks, row_blocks)])
    count = count_ref[0, 0]
    for s in range(slots):
        turned = tiles[s].T
        for r in range(row_blocks):
            keep = jnp.logical_and(rows_ref[s] == r, s < count)
            matrix[s * block : (s + 1) * block, r * block : (r + 1) * block] = turned * jnp.where(
                keep, 1.0, 0.0
            ).astype(jnp.bfloat16)

    def choose(d):
        first_row = (g * n + d) * local_rows
        chooser[d] = jnp.where(
            lax.broadcasted_iota(jnp.int32, (local_rows, part), 0) == seeds[...] - first_row, 1.0, 0.0
        ).astype(jnp.bfloat16)
        right[d, 3 * width :] = jnp.ones((MASS_ROWS, local_rows), jnp.bfloat16)
        left[d, 2 * width :] = jnp.ones((MASS_ROWS, local_rows), jnp.bfloat16)

    def apply(basis):
        picked = jnp.concatenate([basis[columns_ref[s]] for s in range(slots)], axis=1)
        return dot16(picked, matrix[...])

    def start_gram(image, turn):
        gram_dev[turn, me] = pack(mm(image, image, NT))
        return exchange("dev", lambda d, turn=turn: gram_dev.at[turn, d])

    def end_gram(first, turn):
        first.wait_recv()
        gram_group[turn, g] = fold(n, gram_dev.at[turn])
        return exchange("group", lambda d, turn=turn: gram_group.at[turn, d])

    loop(n, choose)
    gather.wait_recv()
    image = apply(basis0)
    first = start_gram(image, 0)
    images0[me] = image
    gather0 = Gather(n, me, lambda d: images0.at[d], [next(used) for _ in range(2)])
    gather0.start()
    second = end_gram(first, 0)
    gather0.relay()
    second.wait_recv()
    inverse = factor_inverse(unpack(fold(m, gram_group.at[0])))
    gather0.wait_recv()

    def solve(d):
        solved = mm(inverse, images0[d])
        for r in range(row_blocks):
            basis1[d * row_blocks + r] = solved[:, r * block : (r + 1) * block].astype(jnp.bfloat16)

    loop(n, solve)
    image = apply(basis1)
    first = start_gram(image, 1)
    images1[me] = image
    gather = Gather(n, me, lambda d: images1.at[d], [next(used) for _ in range(2)])
    gather.start()
    second = end_gram(first, 1)
    gather.relay()
    gather.wait_recv()

    def chosen(d):
        pieces = dot16(jnp.concatenate(three(images1[d]), axis=0), chooser[d])
        return pieces[:width] + pieces[width : 2 * width] + pieces[2 * width :]

    seed_group[g] = total_of(n, chosen)
    seeding = exchange("group", lambda d: seed_group.at[d])
    second.wait_recv()
    inverse = factor_inverse(unpack(fold(m, gram_group.at[1])))

    def spread(mass):
        at = lax.broadcasted_iota(jnp.int32, (MASS_ROWS, part), 0)
        high, low = (v.astype(F32) for v in high_low(mass))
        return jnp.where(at == 0, high, jnp.where(at == 1, low, 0.0)).astype(jnp.bfloat16)

    def normalise(image_t):
        embedding = mm(inverse, image_t) * jnp.sqrt(F32(total_rows))
        return embedding * (1.0 / jnp.sqrt(jnp.sum(embedding * embedding, axis=0, keepdims=True) + 1e-06))

    def embed(d):
        unit = normalise(images1[d])
        units[d] = unit
        square[d] = -SHARPNESS * jnp.sum(unit * unit, axis=0, keepdims=True)
        high, low = high_low(unit)
        for at, piece in enumerate((high, low, high)):
            right[d, at * width : (at + 1) * width] = piece
        left[d, :width] = high
        left[d, width : 2 * width] = low

    loop(n, embed)
    unit_copy = pltpu.make_async_copy(units.at[me], unit_out, out_sems.at[0])
    unit_copy.start()
    seeding.wait_recv()
    centres = normalise(fold(m, seed_group))
    for turn in range(KSTEPS):
        high, low = high_low(2.0 * SHARPNESS * centres)
        bias = [v.astype(F32) for v in three(-SHARPNESS * jnp.sum(centres * centres, axis=0, keepdims=True))]
        bias = jnp.concatenate([*bias, jnp.zeros((MASS_ROWS - len(bias), part), F32)], axis=0).astype(jnp.bfloat16)
        table = jnp.concatenate([high, high, low, bias], axis=0)

        def weigh(d):
            values = jnp.exp(dot16(table, right[d], TN) + square[d])
            weights[d] = values
            weights_scale[pl.ds(d, 1)] = jnp.sum(values, axis=0, keepdims=True)

        loop(n, weigh)
        den[turn, me] = weights_scale[...].astype(jnp.bfloat16)
        exchange("dev", lambda d, turn=turn: den.at[turn, d]).wait_recv()
        units_of = 1.0 / fold(n, den.at[turn])
        weights_scale[...] = units_of

        def gathered(d):
            member = weights[d] * weights_scale[pl.ds(d, 1)]
            return dot16(left[d], member.astype(jnp.bfloat16), NT)

        pair = total_of(n, gathered)
        mass = pair[2 * width : 2 * width + 1]
        sums[turn, g, :width] = (pair[:width] + pair[width : 2 * width]).astype(jnp.bfloat16)
        sums[turn, g, width:] = spread(mass)
        exchange("group", lambda d, turn=turn: sums.at[turn, d]).wait_recv()
        total = fold(m, sums.at[turn])
        centres = total[:width] / (total[width : width + 1] + total[width + 1 : width + 2])
    final[...] = centres.astype(jnp.bfloat16)
    own_copy = pltpu.make_async_copy(final, centres_out.at[me], out_sems.at[1])
    own_copy.start()
    exchange("dev", lambda d: centres_out.at[d], lambda p: final).wait_recv()
    own_copy.wait()
    unit_copy.wait()
    for made in pending:
        made.wait_send()
    gather0.wait_send()
    gather.wait_send()


def widen(n, unit_in, parts, unit_out, centres_out):
    unit_out[...] = unit_in[...]
    centres_out[...] = jnp.concatenate([parts[d].astype(F32) for d in range(n)], axis=1)


def local(tile_values, tile_rows, tile_columns, tile_count, start_basis, seed_rows):
    n, m = lax.axis_size("dev"), lax.axis_size("group")
    slots, block = tile_values.shape[0], tile_values.shape[1]
    local_rows, width = start_basis.shape
    row_blocks = local_rows // block
    clusters = seed_rows.shape[0]
    part = clusters // n
    vmem = pl.BlockSpec(memory_space=pltpu.VMEM)
    anywhere = pl.BlockSpec(memory_space=pl.ANY)
    half = (width // 2, 2 * width)
    B16 = jnp.bfloat16
    axes = ["dev", "dev", "dev", "dev", "group", "dev", "dev", "dev", "group", "group"]
    axes += ["dev", "group"] * KSTEPS + ["dev"]
    sems = []
    for axis in axes:
        sems += [pltpu.SemaphoreType.DMA((n if axis == "dev" else m,))] * 2
    unit, centres = pl.pallas_call(
        functools.partial(kernel, n, m, local_rows * n * m),
        out_shape=(
            pltpu.VMEM((width, local_rows), F32),
            pltpu.VMEM((n, width, part), B16),
        ),
        in_specs=[anywhere] * 6,
        out_specs=(vmem, vmem),
        scratch_shapes=[
            pltpu.VMEM(tile_values.shape, B16),
            pltpu.SMEM(tile_rows.shape, jnp.int32),
            pltpu.SMEM(tile_columns.shape, jnp.int32),
            pltpu.SMEM((1, 1), jnp.int32),
            pltpu.VMEM((1, part), jnp.int32),
            pltpu.VMEM((slots * block, local_rows), B16),
            pltpu.VMEM((n * row_blocks, width, block), B16),
            pltpu.VMEM((n * row_blocks, width, block), B16),
            pltpu.VMEM((n, width, local_rows), F32),
            pltpu.VMEM((n, width, local_rows), F32),
            pltpu.VMEM((2, n, *half), F32),
            pltpu.VMEM((2, m, *half), F32),
            pltpu.VMEM((n, local_rows, part), B16),
            pltpu.VMEM((m, width, part), F32),
            pltpu.VMEM((n, 3 * width + MASS_ROWS, local_rows), B16),
            pltpu.VMEM((n, 2 * width + MASS_ROWS, local_rows), B16),
            pltpu.VMEM((n, 1, local_rows), F32),
            pltpu.VMEM((n, width, local_rows), F32),
            pltpu.VMEM((n, part, local_rows), F32),
            pltpu.VMEM((KSTEPS, n, n, local_rows), B16),
            pltpu.VMEM((n, local_rows), F32),
            pltpu.VMEM((KSTEPS, m, width + MASS_ROWS, part), B16),
            pltpu.VMEM((width, part), B16),
            pltpu.SemaphoreType.DMA((row_blocks + 5,)),
            pltpu.SemaphoreType.DMA((2,)),
            *sems,
        ],
        compiler_params=pltpu.CompilerParams(
            collective_id=0, has_side_effects=True, vmem_limit_bytes=58 * 1024 * 1024
        ),
        name="spectral",
    )(tile_values, tile_rows, tile_columns, tile_count.reshape(1, 1), start_basis.T, seed_rows.reshape(n, 1, part))
    vmem = pl.BlockSpec(memory_space=pltpu.VMEM)
    unit, centres = pl.pallas_call(
        functools.partial(widen, n),
        out_shape=(
            jax.ShapeDtypeStruct((width, local_rows), F32),
            jax.ShapeDtypeStruct((width, clusters), F32),
        ),
        in_specs=[vmem, vmem],
        out_specs=(vmem, vmem),
        name="widen",
    )(pltpu.with_memory_space_constraint(unit, pltpu.VMEM), pltpu.with_memory_space_constraint(centres, pltpu.VMEM))
    return unit.T, centres.T


def solution(mesh):
    return jax.shard_map(
        local,
        mesh=mesh,
        in_specs=(
            P(("group", "dev"), None, None),
            P(("group", "dev")),
            P(("group", "dev")),
            P(("group", "dev")),
            P(("group", "dev"), None),
            P(),
        ),
        out_specs=(P(("group", "dev"), None), P()),
        check_vma=False,
    )
```

```python
import functools

import jax
import jax.numpy as jnp
from jax import lax
from jax.experimental import pallas as pl
from jax.experimental.pallas import tpu as pltpu
from jax.sharding import PartitionSpec as P

KSTEPS = 2
SHARPNESS = 4.0
MASS_ROWS = 16
LANES = 128
MESH = pl.DeviceIdType.MESH
F32 = jnp.float32
HIGHEST = lax.Precision.HIGHEST
NN = (((1,), (0,)), ((), ()))
NT = (((1,), (1,)), ((), ()))
TN = (((0,), (0,)), ((), ()))


def mm(a, b, dims=NN):
    return lax.dot_general(a, b, dims, precision=HIGHEST, preferred_element_type=F32)


def high_low(x):
    high = x.astype(jnp.bfloat16)
    return high, (x - high.astype(F32)).astype(jnp.bfloat16)


def dot16(a, b, dims=NN):
    return lax.dot_general(a, b, dims, preferred_element_type=F32)


def three(x):
    high = x.astype(jnp.bfloat16)
    return (high, *high_low(x - high.astype(F32)))


def loop(n, body):
    if n <= 8:
        for i in range(n):
            body(i)
    else:

        def step(i, carry):
            body(i)
            return carry

        lax.fori_loop(0, n, step, 0)


def fold(n, ref):
    total = ref[0].astype(F32)
    if n <= 8:
        for i in range(1, n):
            total = total + ref[i].astype(F32)
        return total
    return lax.fori_loop(1, n, lambda i, total: total + ref[i].astype(F32), total)


def small(n):
    return n <= 8 and n & (n - 1) == 0


def flip(me, mask):
    out, bit = me, 1
    while bit <= mask:
        if mask & bit:
            out = out + bit - 2 * bit * lax.rem(out // bit, 2)
        bit *= 2
    return out


class Exchange:
    def __init__(self, axis, n, me, land, sems, source=None):
        self.axis, self.n, self.me = axis, n, me
        self.land, self.source = land, source
        self.send, self.recv = sems

    def copy(self, peer, slot):
        source = self.land(self.me) if self.source is None else self.source(peer)
        return pltpu.make_async_remote_copy(
            src_ref=source,
            dst_ref=self.land(slot),
            send_sem=self.send.at[peer],
            recv_sem=self.recv.at[slot],
            device_id={self.axis: peer},
            device_id_type=MESH,
        )

    def peer(self, i):
        if small(self.n):
            return flip(self.me, self.n - 1 - i)
        return lax.rem(self.me + 1 + i, self.n)

    def start(self):
        loop(self.n - 1, lambda i: self.copy(self.peer(i), self.me).start())

    def wait_recv(self):
        loop(self.n - 1, lambda i: self.copy(self.peer(i), self.peer(i)).wait_recv())

    def wait_send(self):
        loop(self.n - 1, lambda i: self.copy(self.peer(i), self.me).wait_send())


def total_of(n, value):
    total = value(0)
    if n <= 8:
        for d in range(1, n):
            total = total + value(d)
        return total
    return lax.fori_loop(1, n, lambda d, total: total + value(d), total)


class Gather:
    def __init__(self, n, me, land, pairs):
        self.n, self.me, self.land = n, me, land
        self.pairs = pairs
        self.twin = self.me + 1 - 2 * lax.rem(self.me, 2)

    def copy(self, owner, slot, to, stage):
        send, recv = self.pairs[stage]
        return pltpu.make_async_remote_copy(
            src_ref=self.land(owner),
            dst_ref=self.land(owner),
            send_sem=send.at[slot],
            recv_sem=recv.at[owner],
            device_id={"dev": to},
            device_id_type=MESH,
        )

    def far(self, i):
        if small(self.n):
            return flip(self.me, 2 * (i + 1))
        return lax.rem(self.me + 2 + 2 * i, self.n)

    def start(self):
        self.copy(self.me, self.me, self.twin, 1).start()
        last = self.n // 2 - 2
        loop(last + 1, lambda i: self.copy(self.me, self.far(last - i), self.far(last - i), 0).start())

    def relay(self):
        def one(i):
            owner = self.far(i)
            self.copy(owner, owner, owner, 0).wait_recv()
            self.copy(owner, owner, self.twin, 1).start()

        loop(self.n // 2 - 1, one)

    def other(self, i):
        return lax.rem(self.twin + 2 * i, self.n)

    def wait_recv(self):
        loop(self.n // 2, lambda i: self.copy(self.other(i), self.other(i), self.twin, 1).wait_recv())

    def wait_send(self):
        self.copy(self.me, self.me, self.twin, 1).wait_send()

        def one(i):
            owner = self.far(i)
            self.copy(self.me, owner, owner, 0).wait_send()
            self.copy(owner, owner, self.twin, 1).wait_send()

        loop(self.n // 2 - 1, one)


def factor_inverse(gram):
    k = gram.shape[0]
    wide = 2 * k
    rows = lax.broadcasted_iota(jnp.int32, (k, k), 0)
    lanes = lax.broadcasted_iota(jnp.int32, (k, k), 1)
    table = jnp.concatenate([gram, jnp.where(rows == lanes, 1.0, 0.0).astype(F32)], axis=1)
    count = k // 8
    parts = [table[8 * b : 8 * b + 8] for b in range(count)]
    sub = lax.broadcasted_iota(jnp.int32, (8, wide), 0)

    def full(v):
        return jnp.broadcast_to(v, (8, wide))

    done = []
    for b in range(count):
        own, at = parts[b], 8 * b
        row = [full(own[s : s + 1]) for s in range(8)]
        cell = [[full(own[s : s + 1, at + r : at + r + 1]) for r in range(s + 1)] for s in range(8)]
        column = {c: [full(parts[c][:, at + r : at + r + 1]) for r in range(8)] for c in range(b + 1, count)}
        over = []
        for r in range(8):
            over.append(1.0 / cell[r][r])
            for s in range(r + 1, 8):
                ratio = cell[s][r] * over[r]
                for t in range(r + 1, s + 1):
                    cell[s][t] = cell[s][t] - ratio * cell[t][r]
                row[s] = row[s] - ratio * row[r]
                for values in column.values():
                    values[s] = values[s] - ratio * values[r]
        for c, values in column.items():
            for r in range(8):
                parts[c] = parts[c] - values[r] * (row[r] * over[r])
        own = row[0] * lax.rsqrt(cell[0][0])
        for s in range(1, 8):
            own = jnp.where(sub == s, row[s] * lax.rsqrt(cell[s][s]), own)
        done.append(own)
    return jnp.concatenate(done, axis=0)[:, k:]


def pack(gram):
    half = gram.shape[0] // 2
    return jnp.concatenate([gram[:half], gram[half:]], axis=1)


def unpack(packed):
    k = packed.shape[1] // 2
    return jnp.concatenate([packed[:, :k], packed[:, k:]], axis=0)


def kernel(
    n, m, total_rows,
    tiles_in, rows_in, columns_in, count_in, start_in, seeds_in,
    unit_out, centres_out,
    tiles, rows_ref, columns_ref, count_ref, seeds,
    matrix, basis0, basis1, images0, images1, gram_dev, gram_group,
    chooser, seed_group, right, left, square, units, weights, den, weights_scale, sums, final,
    in_sems, out_sems, *sems,
):
    me, g = lax.axis_index("dev"), lax.axis_index("group")
    pairs = [(sems[2 * i], sems[2 * i + 1]) for i in range(len(sems) // 2)]
    slots, block = tiles.shape[0], tiles.shape[1]
    width, local_rows = start_in.shape
    row_blocks = local_rows // block
    part = seeds.shape[1]

    barrier = pltpu.get_barrier_semaphore()
    for axis, size, index in (("dev", n, me), ("group", m, g)):
        loop(
            size - 1,
            lambda i: pl.semaphore_signal(
                barrier, inc=1, device_id={axis: lax.rem(index + 1 + i, size)}, device_id_type=MESH
            ),
        )
    loads = [(start_in.at[:, r * block : (r + 1) * block], basis0.at[me * row_blocks + r]) for r in range(row_blocks)]
    loads += [(rows_in, rows_ref), (columns_in, columns_ref), (count_in, count_ref), (seeds_in.at[me], seeds)]
    loads += [(tiles_in, tiles)]
    loads = [pltpu.make_async_copy(a, b, in_sems.at[i]) for i, (a, b) in enumerate(loads)]
    for load in loads:
        load.start()
    for load in loads:
        load.wait()
    pl.semaphore_wait(barrier, n - 1 + m - 1)

    used = iter(pairs)
    pending = []

    def exchange(axis, land, source=None):
        size, index = (n, me) if axis == "dev" else (m, g)
        made = Exchange(axis, size, index, land, next(used), source)
        made.start()
        pending.append(made)
        return made

    gather = exchange("dev", lambda d: basis0.at[pl.ds(d * row_blocks, row_blocks)])
    count = count_ref[0, 0]
    for s in range(slots):
        turned = tiles[s].T
        for r in range(row_blocks):
            keep = jnp.logical_and(rows_ref[s] == r, s < count)
            matrix[s * block : (s + 1) * block, r * block : (r + 1) * block] = turned * jnp.where(
                keep, 1.0, 0.0
            ).astype(jnp.bfloat16)

    def choose(d):
        first_row = (g * n + d) * local_rows
        chooser[d] = jnp.where(
            lax.broadcasted_iota(jnp.int32, (local_rows, part), 0) == seeds[...] - first_row, 1.0, 0.0
        ).astype(jnp.bfloat16)
        right[d, 3 * width :] = jnp.ones((MASS_ROWS, local_rows), jnp.bfloat16)
        left[d, 2 * width :] = jnp.ones((MASS_ROWS, local_rows), jnp.bfloat16)

    def apply(basis):
        picked = jnp.concatenate([basis[columns_ref[s]] for s in range(slots)], axis=1)
        return dot16(picked, matrix[...])

    def start_gram(image, turn):
        gram_dev[turn, me] = pack(mm(image, image, NT))
        return exchange("dev", lambda d, turn=turn: gram_dev.at[turn, d])

    def end_gram(first, turn):
        first.wait_recv()
        gram_group[turn, g] = fold(n, gram_dev.at[turn])
        return exchange("group", lambda d, turn=turn: gram_group.at[turn, d])

    loop(n, choose)
    gather.wait_recv()
    image = apply(basis0)
    first = start_gram(image, 0)
    images0[me] = image
    gather0 = Gather(n, me, lambda d: images0.at[d], [next(used) for _ in range(2)])
    gather0.start()
    second = end_gram(first, 0)
    gather0.relay()
    second.wait_recv()
    inverse = factor_inverse(unpack(fold(m, gram_group.at[0])))
    gather0.wait_recv()

    def solve(d):
        solved = mm(inverse, images0[d])
        for r in range(row_blocks):
            basis1[d * row_blocks + r] = solved[:, r * block : (r + 1) * block].astype(jnp.bfloat16)

    loop(n, solve)
    image = apply(basis1)
    first = start_gram(image, 1)
    images1[me] = image
    gather = Gather(n, me, lambda d: images1.at[d], [next(used) for _ in range(2)])
    gather.start()
    second = end_gram(first, 1)
    gather.relay()
    gather.wait_recv()

    def chosen(d):
        pieces = dot16(jnp.concatenate(three(images1[d]), axis=0), chooser[d])
        return pieces[:width] + pieces[width : 2 * width] + pieces[2 * width :]

    seed_group[g] = total_of(n, chosen)
    seeding = exchange("group", lambda d: seed_group.at[d])
    second.wait_recv()
    inverse = factor_inverse(unpack(fold(m, gram_group.at[1])))

    def spread(mass):
        at = lax.broadcasted_iota(jnp.int32, (MASS_ROWS, part), 0)
        high, low = (v.astype(F32) for v in high_low(mass))
        return jnp.where(at == 0, high, jnp.where(at == 1, low, 0.0)).astype(jnp.bfloat16)

    def normalise(image_t):
        embedding = mm(inverse, image_t) * jnp.sqrt(F32(total_rows))
        return embedding * lax.rsqrt(jnp.sum(embedding * embedding, axis=0, keepdims=True) + 1e-06)

    def embed(d):
        unit = normalise(images1[d])
        units[d] = unit
        square[d] = -SHARPNESS * jnp.sum(unit * unit, axis=0, keepdims=True)
        high, low = high_low(unit)
        for at, piece in enumerate((high, low, high)):
            right[d, at * width : (at + 1) * width] = piece
        left[d, :width] = high
        left[d, width : 2 * width] = low

    loop(n, embed)
    unit_copy = pltpu.make_async_copy(units.at[me], unit_out, out_sems.at[0])
    unit_copy.start()
    seeding.wait_recv()
    centres = normalise(fold(m, seed_group))
    for turn in range(KSTEPS):
        high, low = high_low(2.0 * SHARPNESS * centres)
        bias = [v.astype(F32) for v in three(-SHARPNESS * jnp.sum(centres * centres, axis=0, keepdims=True))]
        bias = jnp.concatenate([*bias, jnp.zeros((MASS_ROWS - len(bias), part), F32)], axis=0).astype(jnp.bfloat16)
        table = jnp.concatenate([high, high, low, bias], axis=0)

        def weigh(d):
            values = jnp.exp(dot16(table, right[d], TN) + square[d])
            weights[d] = values
            weights_scale[pl.ds(d, 1)] = jnp.sum(values, axis=0, keepdims=True)

        loop(n, weigh)
        den[turn, me] = weights_scale[...].astype(jnp.bfloat16)
        exchange("dev", lambda d, turn=turn: den.at[turn, d]).wait_recv()
        units_of = 1.0 / fold(n, den.at[turn])
        weights_scale[...] = units_of

        def gathered(d):
            member = weights[d] * weights_scale[pl.ds(d, 1)]
            return dot16(left[d], member.astype(jnp.bfloat16), NT)

        pair = total_of(n, gathered)
        mass = pair[2 * width : 2 * width + 1]
        sums[turn, g, :width] = (pair[:width] + pair[width : 2 * width]).astype(jnp.bfloat16)
        sums[turn, g, width:] = spread(mass)
        exchange("group", lambda d, turn=turn: sums.at[turn, d]).wait_recv()
        total = fold(m, sums.at[turn])
        centres = total[:width] / (total[width : width + 1] + total[width + 1 : width + 2])
    final[...] = centres.astype(jnp.bfloat16)
    own_copy = pltpu.make_async_copy(final, centres_out.at[me], out_sems.at[1])
    own_copy.start()
    exchange("dev", lambda d: centres_out.at[d], lambda p: final).wait_recv()
    own_copy.wait()
    unit_copy.wait()
    for made in pending:
        made.wait_send()
    gather0.wait_send()
    gather.wait_send()


def widen(n, unit_in, parts, unit_out, centres_out):
    unit_out[...] = unit_in[...]
    centres_out[...] = jnp.concatenate([parts[d].astype(F32) for d in range(n)], axis=1)


def local(tile_values, tile_rows, tile_columns, tile_count, start_basis, seed_rows):
    n, m = lax.axis_size("dev"), lax.axis_size("group")
    slots, block = tile_values.shape[0], tile_values.shape[1]
    local_rows, width = start_basis.shape
    row_blocks = local_rows // block
    clusters = seed_rows.shape[0]
    part = clusters // n
    vmem = pl.BlockSpec(memory_space=pltpu.VMEM)
    anywhere = pl.BlockSpec(memory_space=pl.ANY)
    half = (width // 2, 2 * width)
    B16 = jnp.bfloat16
    axes = ["dev", "dev", "dev", "dev", "group", "dev", "dev", "dev", "group", "group"]
    axes += ["dev", "group"] * KSTEPS + ["dev"]
    sems = []
    for axis in axes:
        sems += [pltpu.SemaphoreType.DMA((n if axis == "dev" else m,))] * 2
    unit, centres = pl.pallas_call(
        functools.partial(kernel, n, m, local_rows * n * m),
        out_shape=(
            pltpu.VMEM((width, local_rows), F32),
            pltpu.VMEM((n, width, part), B16),
        ),
        in_specs=[anywhere] * 6,
        out_specs=(vmem, vmem),
        scratch_shapes=[
            pltpu.VMEM(tile_values.shape, B16),
            pltpu.SMEM(tile_rows.shape, jnp.int32),
            pltpu.SMEM(tile_columns.shape, jnp.int32),
            pltpu.SMEM((1, 1), jnp.int32),
            pltpu.VMEM((1, part), jnp.int32),
            pltpu.VMEM((slots * block, local_rows), B16),
            pltpu.VMEM((n * row_blocks, width, block), B16),
            pltpu.VMEM((n * row_blocks, width, block), B16),
            pltpu.VMEM((n, width, local_rows), F32),
            pltpu.VMEM((n, width, local_rows), F32),
            pltpu.VMEM((2, n, *half), F32),
            pltpu.VMEM((2, m, *half), F32),
            pltpu.VMEM((n, local_rows, part), B16),
            pltpu.VMEM((m, width, part), F32),
            pltpu.VMEM((n, 3 * width + MASS_ROWS, local_rows), B16),
            pltpu.VMEM((n, 2 * width + MASS_ROWS, local_rows), B16),
            pltpu.VMEM((n, 1, local_rows), F32),
            pltpu.VMEM((n, width, local_rows), F32),
            pltpu.VMEM((n, part, local_rows), F32),
            pltpu.VMEM((KSTEPS, n, n, local_rows), B16),
            pltpu.VMEM((n, local_rows), F32),
            pltpu.VMEM((KSTEPS, m, width + MASS_ROWS, part), B16),
            pltpu.VMEM((width, part), B16),
            pltpu.SemaphoreType.DMA((row_blocks + 5,)),
            pltpu.SemaphoreType.DMA((2,)),
            *sems,
        ],
        compiler_params=pltpu.CompilerParams(
            collective_id=0, has_side_effects=True, vmem_limit_bytes=58 * 1024 * 1024
        ),
        name="spectral",
    )(tile_values, tile_rows, tile_columns, tile_count.reshape(1, 1), start_basis.T, seed_rows.reshape(n, 1, part))
    vmem = pl.BlockSpec(memory_space=pltpu.VMEM)
    unit, centres = pl.pallas_call(
        functools.partial(widen, n),
        out_shape=(
            jax.ShapeDtypeStruct((width, local_rows), F32),
            jax.ShapeDtypeStruct((width, clusters), F32),
        ),
        in_specs=[vmem, vmem],
        out_specs=(vmem, vmem),
        name="widen",
    )(pltpu.with_memory_space_constraint(unit, pltpu.VMEM), pltpu.with_memory_space_constraint(centres, pltpu.VMEM))
    return unit.T, centres.T


def solution(mesh):
    return jax.shard_map(
        local,
        mesh=mesh,
        in_specs=(
            P(("group", "dev"), None, None),
            P(("group", "dev")),
            P(("group", "dev")),
            P(("group", "dev")),
            P(("group", "dev"), None),
            P(),
        ),
        out_specs=(P(("group", "dev"), None), P()),
        check_vma=False,
    )
```
